32 devices in a mesh: dom: 8 (over z, x), rep: 4 (over y, core).
Axes of the slice: x: 2, y: 2, z: 4, core: 2. Of those that a mesh axis runs over, the one named last changes fastest.
Arguments:
- features: bfloat16 [2048, 256], P('dom'), may hold values from -6 to 6
- positions: float32 [3, 2048], P(None, 'dom'), may hold values from -6 to 6
- radial: bfloat16 [8, 256, 256], replicated, may hold values from -0.03125 to 0.03125
- mixing: bfloat16 [256, 256], replicated, may hold values from -0.375 to 0.375
- readout: float32 [256], replicated, may hold values from -4 to 4
- decay: float32 [8], replicated, may hold values from 0.1 to 1
- send_rows: int32 [4, 1024], P(None, 'dom'), may hold values from 0 to 255
- pair_home: int32 [1536], P(('dom', 'rep')), may hold values from 0 to 1
- pair_other: int32 [1536], P(('dom', 'rep')), may hold values from 0 to 5
- pair_kind: int32 [1536], P(('dom', 'rep')), may hold values from 0 to 7
- pair_image: int32 [3, 1536], P(None, ('dom', 'rep')), may hold values from -1 to 1
Outputs:
- grad_features: bfloat16 [2048, 256], P('dom')
- forces: float32 [3, 2048], P(None, 'dom')
- virials: float32 [6, 2048], P(None, 'dom')
- grad_mixing: float32 [256, 256], P('dom', 'rep')
The draws below stay inside these ranges and needn't reach their ends.
Inputs may be any that keep to these rules, and one draw needn't show every extreme that they name: `send_rows`: rows may repeat within a round.
All inputs are finite; a program needn't handle non-finite values.
Results may differ from the reference program's by a relative error of at most 0.006.
Values may be sent and summed in bfloat16 or wider, within the bound.
A program may use at most 128 MiB of HBM per device.

```python
import math
import jax
import jax.numpy as jnp
from jax import lax

C = 256
RADIAL = 8
TILE_ATOMS = 128
ROUNDS = 4
SUBDOMAIN_ATOMS = 256
PAIRS_DEV = 48
NATOM = 2048
PAIRS = 1536
N_DOM = 8
N_REP = 4


def plant(array, key, smallest, top_value):
    place = [jax.random.randint(jax.random.fold_in(key, axis), (), 0, length) for axis, length in enumerate(array.shape)]
    widest = array.shape.index(max(array.shape))
    next_to = place[:widest] + [(place[widest] + 1) % array.shape[widest]] + place[widest + 1:]
    return array.at[tuple(place)].set(smallest).at[tuple(next_to)].set(top_value)


def steps_of(own_key, extent, cuts, least, top_value):
    def one(position, blocks):
        steps = jax.random.uniform(jax.random.fold_in(jax.random.fold_in(own_key, 6), position), (blocks,), jnp.float32, least / len(cuts), top_value / len(cuts))
        return jnp.repeat(jnp.exp(steps), extent[position] // blocks).reshape((-1,) + (1,) * (len(extent) - position - 1))

    level = one(*cuts[0])
    for cut in cuts[1:]:
        level = level * one(*cut)
    return level


def scatter_about(own_key, dims, spread, bound, split=(), dtype=jnp.bfloat16):
    loudness = steps_of(own_key, dims, split, -0.22, 0.18) if split else 1.0
    entries = jax.random.normal(own_key, dims, jnp.float32) * spread * loudness
    return jnp.minimum(jnp.maximum(entries, -bound), bound).astype(dtype)


def setup_inputs(seed: int = 0) -> dict:
    arg_keys = jax.random.split(jax.random.key(seed), 12)
    return {
        "features": scatter_about(arg_keys[0], (NATOM, C), 1.0, 6.0, ((0, 8),)),
        "positions": scatter_about(arg_keys[1], (3, NATOM), 1.0, 6.0, ((1, 8),), jnp.float32),
        "radial": scatter_about(arg_keys[2], (RADIAL, C, C), (C * TILE_ATOMS) ** -0.5, 0.03125),
        "mixing": scatter_about(arg_keys[3], (C, C), C ** -0.5, 0.375),
        "readout": scatter_about(arg_keys[4], (C,), 1.0, 4.0, (), jnp.float32),
        "decay": jnp.clip(jnp.exp(jax.random.uniform(arg_keys[5], (RADIAL,), jnp.float32, math.log(0.1), math.log(1.0))), 0.1, 1.0),
        "send_rows": plant(jax.random.randint(arg_keys[6], (ROUNDS, TILE_ATOMS * N_DOM), 0, SUBDOMAIN_ATOMS), jax.random.fold_in(arg_keys[6], 1), 0, SUBDOMAIN_ATOMS - 1).astype(jnp.int32),
        "pair_home": plant(jax.random.randint(arg_keys[7], (PAIRS,), 0, SUBDOMAIN_ATOMS // TILE_ATOMS), jax.random.fold_in(arg_keys[7], 1), 0, (SUBDOMAIN_ATOMS // TILE_ATOMS) - 1).astype(jnp.int32),
        "pair_other": plant(jax.random.randint(arg_keys[8], (PAIRS,), 0, SUBDOMAIN_ATOMS // TILE_ATOMS + ROUNDS), jax.random.fold_in(arg_keys[8], 1), 0, (SUBDOMAIN_ATOMS // TILE_ATOMS + ROUNDS) - 1).astype(jnp.int32),
        "pair_kind": plant(jax.random.randint(arg_keys[9], (PAIRS,), 0, RADIAL), jax.random.fold_in(arg_keys[9], 1), 0, RADIAL - 1).astype(jnp.int32),
        "pair_image": plant(jax.random.randint(arg_keys[10], (3, PAIRS), -1, 2), jax.random.fold_in(arg_keys[10], 1), -1, 1).astype(jnp.int32),
    }


offsets = (1, -1, 2, -2)
cell_edge = 2.0
component_pairs = ((0, 0), (1, 1), (2, 2), (0, 1), (0, 2), (1, 2))
highest_precision = lax.Precision.HIGHEST


def lowered(values):
    return lax.optimization_barrier(values.astype(jnp.bfloat16)).astype(jnp.float32)


def pair_setup(ext_feat, ext_pos, home_tile, other_tile, radial_pick, image_shift, radial, decay):
    tiles_feat = ext_feat.reshape(-1, TILE_ATOMS, ext_feat.shape[1])
    tiles_pos = ext_pos.reshape(3, -1, TILE_ATOMS)
    far_end = jnp.take(tiles_pos, other_tile, axis=1) + image_shift[:, :, None].astype(jnp.float32) * cell_edge
    near_end = jnp.take(tiles_pos, home_tile, axis=1)
    separation = far_end[:, :, None, :] - near_end[:, :, :, None]
    rates = jnp.take(decay, radial_pick)
    kernel = jnp.exp(-rates[:, None, None] * jnp.sum(separation * separation, axis=0))
    partner_rows = jnp.take(tiles_feat, other_tile, axis=0).astype(jnp.float32)
    chosen = jnp.take(radial, radial_pick, axis=0).astype(jnp.float32)
    mapped = lowered(jnp.einsum('pbc,pcd->pbd', partner_rows, chosen, precision=highest_precision))
    return separation, rates, kernel, mapped, chosen


def reference(features, positions, radial, mixing, readout, decay, send_rows, pair_home, pair_other, pair_kind, pair_image):
    channel_count = features.shape[1]
    home_tiles = SUBDOMAIN_ATOMS // TILE_ATOMS
    extended_tiles = home_tiles + ROUNDS
    pair_count = PAIRS_DEV * N_REP
    domain_feat = features.reshape(N_DOM, SUBDOMAIN_ATOMS, channel_count)
    domain_pos = positions.reshape(3, N_DOM, SUBDOMAIN_ATOMS).transpose(1, 0, 2)
    send_table = send_rows.reshape(ROUNDS, N_DOM, TILE_ATOMS)
    halo_feat = []
    halo_pos = []
    for section_no in range(ROUNDS):
        picked_feat = jnp.take_along_axis(domain_feat, send_table[section_no][:, :, None], axis=1)
        picked_pos = jnp.take_along_axis(domain_pos, send_table[section_no][:, None, :], axis=2)
        halo_feat.append(jnp.roll(picked_feat, offsets[section_no], axis=0))
        halo_pos.append(jnp.roll(picked_pos, offsets[section_no], axis=0))
    ext_feat = jnp.concatenate([domain_feat] + halo_feat, axis=1)
    ext_pos = jnp.concatenate([domain_pos] + halo_pos, axis=2)
    home_tile = pair_home.reshape(N_DOM, pair_count)
    other_tile = pair_other.reshape(N_DOM, pair_count)
    radial_pick = pair_kind.reshape(N_DOM, pair_count)
    image_shift = pair_image.reshape(3, N_DOM, pair_count).transpose(1, 0, 2)
    home_iota = lax.iota(jnp.int32, home_tiles)
    ext_iota = lax.iota(jnp.int32, extended_tiles)

    def forward_domain(inputs):
        feat_one, pos_one, home_one, other_one, pick_one, shift_one = inputs
        separation, rates, kernel, mapped, chosen = pair_setup(feat_one, pos_one, home_one, other_one, pick_one, shift_one, radial, decay)
        message_rows = jnp.einsum('pab,pbd->pad', lowered(kernel), mapped, precision=highest_precision)
        home_lookup_table = (home_one[None, :] == home_iota[:, None]).astype(jnp.float32)
        return jnp.einsum('so,oxe->sxe', home_lookup_table, message_rows, precision=highest_precision).reshape(SUBDOMAIN_ATOMS, channel_count)

    message = lax.map(forward_domain, (ext_feat, ext_pos, home_tile, other_tile, radial_pick, image_shift))
    message = message.reshape(NATOM, channel_count)
    packed = message.astype(jnp.bfloat16)
    mixed_rows = jnp.dot(packed, mixing, preferred_element_type=jnp.float32)
    sigmoid_rows = jax.nn.sigmoid(mixed_rows)
    slope_rows = (readout * sigmoid_rows * (1.0 + mixed_rows * (1.0 - sigmoid_rows))).astype(jnp.bfloat16)
    adjoint = jnp.dot(slope_rows, mixing.T, preferred_element_type=jnp.float32).astype(jnp.bfloat16)
    grad_mixing = jnp.dot(packed.T, slope_rows, preferred_element_type=jnp.float32)
    adjoint_dom = adjoint.reshape(N_DOM, SUBDOMAIN_ATOMS, channel_count)

    def backward_domain(inputs):
        feat_one, pos_one, home_one, other_one, pick_one, shift_one, adjoint_one = inputs
        separation, rates, kernel, mapped, chosen = pair_setup(feat_one, pos_one, home_one, other_one, pick_one, shift_one, radial, decay)
        kernel_low = lowered(kernel)
        adjoint_tiles = jnp.take(adjoint_one.reshape(home_tiles, TILE_ATOMS, channel_count), home_one, axis=0).astype(jnp.float32)
        kernel_grad = jnp.einsum('pad,pbd->pab', adjoint_tiles, mapped, precision=highest_precision)
        mapped_grad = lowered(jnp.einsum('pab,pad->pbd', kernel_low, adjoint_tiles, precision=highest_precision))
        feature_grad = jnp.einsum('pbd,pcd->pbc', mapped_grad, chosen, precision=highest_precision)
        weight = -2.0 * rates[:, None, None] * kernel * kernel_grad
        home_atom_side = []
        partner_side = []
        for axis_one in range(3):
            pull = weight * separation[axis_one]
            home_atom_side.append(jnp.sum(pull, axis=2))
            partner_side.append(-jnp.sum(pull, axis=1))
        for axis_one, axis_two in component_pairs:
            product = weight * separation[axis_one] * separation[axis_two]
            home_atom_side.append(-0.5 * jnp.sum(product, axis=2))
            partner_side.append(-0.5 * jnp.sum(product, axis=1))
        home_atom_side = jnp.stack(home_atom_side)
        partner_side = jnp.stack(partner_side)
        home_lookup_table = (home_one[None, :] == home_iota[:, None]).astype(jnp.float32)
        partner_table = (other_one[None, :] == ext_iota[:, None]).astype(jnp.float32)
        ext_grad = jnp.einsum('jp,pbc->jbc', partner_table, feature_grad, precision=highest_precision).reshape(extended_tiles * TILE_ATOMS, channel_count)
        extended_side = jnp.einsum('it,ztq->ziq', partner_table, partner_side, precision=highest_precision).reshape(9, extended_tiles * TILE_ATOMS)
        self_side = jnp.einsum('qk,gkv->gqv', home_lookup_table, home_atom_side, precision=highest_precision).reshape(9, SUBDOMAIN_ATOMS) + extended_side[:, :SUBDOMAIN_ATOMS]
        return ext_grad[:SUBDOMAIN_ATOMS], self_side, ext_grad[SUBDOMAIN_ATOMS:], extended_side[:, SUBDOMAIN_ATOMS:]

    own_grad, self_side, halo_grad, halo_side = lax.map(backward_domain, (ext_feat, ext_pos, home_tile, other_tile, radial_pick, image_shift, adjoint_dom))
    atom_iota = lax.iota(jnp.int32, SUBDOMAIN_ATOMS)
    for section_no in range(ROUNDS):
        returned_grad = jnp.roll(halo_grad[:, section_no * TILE_ATOMS:(section_no + 1) * TILE_ATOMS], -offsets[section_no], axis=0)
        returned_side = jnp.roll(halo_side[:, :, section_no * TILE_ATOMS:(section_no + 1) * TILE_ATOMS], -offsets[section_no], axis=0)
        send_onehot = (send_table[section_no][:, :, None] == atom_iota[None, None, :]).astype(jnp.float32)
        own_grad = own_grad + jnp.einsum('dta,dtc->dac', send_onehot, returned_grad, precision=highest_precision)
        self_side = self_side + jnp.einsum('dta,dct->dca', send_onehot, returned_side, precision=highest_precision)
    grad_features = own_grad.reshape(NATOM, channel_count).astype(jnp.bfloat16)
    forces = self_side[:, :3].transpose(1, 0, 2).reshape(3, NATOM)
    virials = self_side[:, 3:].transpose(1, 0, 2).reshape(6, NATOM)
    return grad_features, forces, virials, grad_mixing
```

```python
import functools

import jax
import jax.numpy as jnp
from jax import lax
from jax.experimental import pallas as pl
from jax.experimental.pallas import tpu as pltpu
from jax.sharding import PartitionSpec as P

TILE = 128
OFFSETS = (1, -1, 2, -2)
CELL = 2.0
GROUP = 4
F32 = jnp.float32
BF16 = jnp.bfloat16
MESH = pl.DeviceIdType.MESH
VMEM = pl.BlockSpec(memory_space=pltpu.VMEM)
SMEM = pl.BlockSpec(memory_space=pltpu.SMEM)


def nt(a, b):
    return lax.dot_general(a, b, (((1,), (1,)), ((), ())), preferred_element_type=F32)


def tn(a, b):
    return lax.dot_general(a, b, (((0,), (0,)), ((), ())), preferred_element_type=F32)


def mm(a, b):
    return jnp.dot(a, b, preferred_element_type=F32)


def split3(x):
    hi = x.astype(BF16)
    rest = x - hi.astype(F32)
    mid = rest.astype(BF16)
    low = (rest - mid.astype(F32)).astype(BF16)
    return hi, mid, low


def halo_kernel(n_dom, feat, pos, rows, radial, mapped, tiles, sendf, sendp, recvf, recvp,
                sf, sp, rf, rp):
    d = lax.axis_index("dom")
    r = lax.axis_index("rep")
    barrier = pltpu.get_barrier_semaphore()
    for o in OFFSETS:
        pl.semaphore_signal(barrier, inc=1, device_id={"dom": lax.rem(d + o + n_dom, n_dom), "rep": r},
                            device_id_type=MESH)
    atoms = feat.shape[0]
    iota = lax.broadcasted_iota(jnp.int32, (atoms, TILE), 0)
    for t in range(4):
        hot = (iota == rows[t:t + 1, :]).astype(F32)
        sendf[t] = tn(hot.astype(BF16), feat[...]).astype(BF16)
        sendp[t] = jnp.dot(pos[...], hot, precision=lax.Precision.HIGHEST, preferred_element_type=F32)
    pl.semaphore_wait(barrier, 4)
    copies = []
    for t, o in enumerate(OFFSETS):
        to = {"dom": lax.rem(d + o + n_dom, n_dom), "rep": r}
        cf = pltpu.make_async_remote_copy(sendf.at[t], recvf.at[t], sf.at[t], rf.at[t],
                                          device_id=to, device_id_type=MESH)
        cp = pltpu.make_async_remote_copy(sendp.at[t], recvp.at[t], sp.at[t], rp.at[t],
                                          device_id=to, device_id_type=MESH)
        cf.start()
        cp.start()
        copies.append((cf, cp))
    own = atoms // TILE
    for j in range(own):
        tiles[j] = pos[:, j * TILE:(j + 1) * TILE]

    def local(k, _):
        res = mm(feat[...], radial[k]).astype(BF16)
        for j in range(own):
            mapped[j, k] = res[j * TILE:(j + 1) * TILE]
        return 0

    lax.fori_loop(0, radial.shape[0], local, 0)
    for h in range(2):
        for t in (2 * h, 2 * h + 1):
            copies[t][0].wait_recv()
            copies[t][1].wait_recv()
            tiles[own + t] = recvp[t]

        def far(k, _):
            both = jnp.concatenate([recvf[2 * h], recvf[2 * h + 1]], axis=0)
            res = mm(both, radial[k]).astype(BF16)
            mapped[own + 2 * h, k] = res[:TILE]
            mapped[own + 2 * h + 1, k] = res[TILE:]
            return 0

        lax.fori_loop(0, radial.shape[0], far, 0)
    for cf, cp in copies:
        cf.wait_send()
        cp.wait_send()


def forward_kernel(decay, home, other, kind, image, tiles, mapped, out, near, acc):
    for i in range(2):
        for c in range(3):
            near[i, c] = jnp.transpose(jnp.broadcast_to(tiles[i][c:c + 1, :], (TILE, TILE)))
    acc[...] = jnp.zeros_like(acc)

    def body(g, _):
        found = []
        for u in range(GROUP):
            p = g * GROUP + u
            h, o, k = home[p], other[p], kind[p]
            rate = decay[k]
            row = tiles[o]
            d2 = None
            for c in range(3):
                sep = (row[c:c + 1, :] + image[c, p].astype(F32) * CELL) - near[h, c]
                d2 = sep * sep if d2 is None else d2 + sep * sep
            kern = jnp.exp(d2 * (-rate)).astype(BF16)
            found.append((h, mm(kern, mapped[o, k])))
        for h, m in found:
            acc[h] += m
        return 0

    lax.fori_loop(0, home.shape[0] // GROUP, body, 0)
    share = out.shape[1]
    per = TILE // share
    for i in range(2):
        for q in range(per):
            out[i * per + q] = acc[i, q * share:(q + 1) * share, :].astype(BF16)


def atom_kernel(n_rep, msg, mixing, readout, packed, slope, adjoint, recv, pk, sl, s1, r1, s2, r2, s3, r3):
    d = lax.axis_index("dom")
    r = lax.axis_index("rep")
    barrier = pltpu.get_barrier_semaphore()
    peers = [lax.rem(r + i, n_rep) for i in range(1, n_rep)]
    for q in peers:
        pl.semaphore_signal(barrier, inc=1, device_id={"dom": d, "rep": q}, device_id_type=MESH)
    pl.semaphore_wait(barrier, n_rep - 1)

    def push(src, dst, ss, rs, q):
        copy = pltpu.make_async_remote_copy(src, dst, ss, rs, device_id={"dom": d, "rep": q},
                                            device_id_type=MESH)
        copy.start()
        return copy

    def take(dst, ss, rs, q):
        pltpu.make_async_remote_copy(dst, dst, ss, rs, device_id={"dom": d, "rep": q},
                                     device_id_type=MESH).wait_recv()

    sent = [push(msg.at[q], recv.at[r], s1.at[i], r1.at[r], q) for i, q in enumerate(peers)]
    total = msg[r].astype(F32)
    for i, q in enumerate(peers):
        take(recv.at[q], s1.at[i], r1.at[q], q)
        total = total + recv[q].astype(F32)
    low = total.astype(BF16)
    pk[r] = low
    sent += [push(pk.at[r], pk.at[r], s2.at[i], r2.at[r], q) for i, q in enumerate(peers)]
    mixed = mm(low, mixing[...])
    sig = jax.nn.sigmoid(mixed)
    sl[r] = (readout[...] * sig * (1.0 + mixed * (1.0 - sig))).astype(BF16)
    sent += [push(sl.at[r], sl.at[r], s3.at[i], r3.at[r], q) for i, q in enumerate(peers)]
    for i, q in enumerate(peers):
        take(sl.at[q], s3.at[i], r3.at[q], q)
    full = sl[...].reshape(-1, mixing.shape[0])
    slope[...] = full
    adj = nt(full, mixing[...]).astype(BF16)
    for j in range(adjoint.shape[0]):
        adjoint[j] = adj[j * TILE:(j + 1) * TILE]
    for i, q in enumerate(peers):
        take(pk.at[q], s2.at[i], r2.at[q], q)
    packed[...] = pk[...].reshape(-1, mixing.shape[0])
    for copy in sent:
        copy.wait_send()


def backward_kernel(n_rep, decay, home, other, kind, image, tiles, mapped, adjoint, radial, packed, slope,
                    gfeat, side, mix, far, moments, first, second, acc):
    n_ext = tiles.shape[0]
    for j in range(n_ext):
        pos = tiles[j]
        x, y, z = pos[0:1, :], pos[1:2, :], pos[2:3, :]
        for c in range(3):
            far[j, c] = jnp.transpose(jnp.broadcast_to(pos[c:c + 1, :], (TILE, TILE)))
        zero = jnp.zeros((2, TILE), F32)
        one_rows = jnp.concatenate([x, y, z, x, x, y, zero], axis=0)
        two_rows = jnp.concatenate([x, y, z, y, z, z, zero], axis=0)
        first[j] = one_rows
        second[j] = two_rows
        stack = jnp.concatenate([one_rows * two_rows, one_rows, two_rows], axis=0)
        parts = [v.astype(F32) for v in split3(stack)]
        moments[j] = jnp.concatenate(
            [parts[0], jnp.ones((8, TILE), F32), parts[1], parts[2]], axis=0).astype(BF16)
    acc[...] = jnp.zeros_like(acc)
    side[...] = jnp.zeros_like(side)
    sub = lax.broadcasted_iota(jnp.int32, (8, TILE), 0)

    def rows_of(a, b):
        return ((sub == a[0]) | (sub == a[1]) | (sub == a[2])), ((sub == b[0]) | (sub == b[1]))

    is_x1, is_y1 = rows_of((0, 3, 4), (1, 5))
    is_x2, is_y2 = (sub == 0), ((sub == 1) | (sub == 3))

    def fold(res):
        quad = res[0:8] + res[32:40] + res[56:64]
        lin1 = res[8:16] + res[40:48] + res[64:72]
        lin2 = res[16:24] + res[48:56] + res[72:80]
        return quad, lin1, lin2, res[24:32]

    def combine(res, a, b):
        quad, lin1, lin2, one = fold(res)
        force = lin1 - a * one
        virial = -0.5 * (quad - a * lin2 - b * lin1 + a * b * one)
        return jnp.concatenate([force, virial], axis=0)

    def body(g, _):
        found = []
        for u in range(GROUP):
            p = g * GROUP + u
            h, o, k = home[p], other[p], kind[p]
            rate = decay[k]
            shift = [image[c, p].astype(F32) * CELL for c in range(3)]
            row = tiles[h]
            d2 = None
            for c in range(3):
                sep = far[o, c] - (row[c:c + 1, :] - shift[c])
                d2 = sep * sep if d2 is None else d2 + sep * sep
            kern = jnp.exp(d2 * (-rate))
            adj = adjoint[h]
            weight = (-2.0 * rate) * kern * nt(mapped[o, k], adj)
            back = mm(kern.astype(BF16), adj).astype(BF16)
            part = nt(back, radial[k])
            hi = weight.astype(BF16)
            lo = (weight - hi.astype(F32)).astype(BF16)
            near_res = mm(moments[o], hi) + mm(moments[o], lo)
            far_res = nt(moments[h], hi) + nt(moments[h], lo)
            s1 = jnp.where(is_x1, shift[0], jnp.where(is_y1, shift[1], shift[2]))
            s2 = jnp.where(is_x2, shift[0], jnp.where(is_y2, shift[1], shift[2]))
            near_side = combine(near_res, first[h] - s1, second[h] - s2)
            far_side = combine(far_res, first[o] + s1, second[o] + s2)
            found.append((h, o, part, near_side, far_side))
        for h, o, part, near_side, far_side in found:
            acc[o] += part
            side[h] += near_side
            side[o] += far_side
        return 0

    lax.fori_loop(0, home.shape[0] // GROUP, body, 0)
    for j in range(n_ext):
        for half in range(2):
            gfeat[j, half] = acc[j, :, half * TILE:(half + 1) * TILE].astype(BF16)
    r = lax.axis_index("rep")
    channels = slope.shape[1]
    share = channels // n_rep
    pick = (lax.broadcasted_iota(jnp.int32, (channels, share), 0)
            == lax.broadcasted_iota(jnp.int32, (channels, share), 1) + r * share).astype(BF16)
    cols = mm(slope[...], pick).astype(BF16)
    res = tn(packed[...], cols)
    mix[...] = res.reshape(mix.shape)


TILE_CORE = (0, 1, 0, 0, 1, 1)
TILE_SLOT = (0, 0, 1, 2, 1, 2)


def return_kernel(n_dom, n_rep, gfeat, side, mix, rows, out_feat, out_force, out_virial, out_mix,
                  rf, rs, rm, part, pside, qside,
                  sem_sf, sem_rf, sem_ss, sem_rs, sem_sm, sem_rm, sem_sp, sem_rp, sem_sq, sem_rq):
    d = lax.axis_index("dom")
    r = lax.axis_index("rep")
    y = lax.div(r, 2)
    c = lax.rem(r, 2)

    def dom_at(o):
        return lax.rem(d + o + n_dom, n_dom)

    barrier = pltpu.get_barrier_semaphore()

    def hello(dom, rep):
        pl.semaphore_signal(barrier, inc=1, device_id={"dom": dom, "rep": rep}, device_id_type=MESH)

    mine = [(c + 1), -(c + 1)]
    peers = [lax.rem(r + i, n_rep) for i in range(1, n_rep)]
    for o in mine:
        for q in range(n_rep):
            hello(dom_at(o), q)
    for q in peers:
        hello(d, q)

    def greet(i, _):
        hello(lax.rem(d + i, n_dom), r)
        return 0

    lax.fori_loop(1, n_dom, greet, 0)
    pl.semaphore_wait(barrier, 2 * n_rep + n_rep - 1 + n_dom - 1)

    sends = []
    for j in (2, 3, 4, 5, 0, 1):
        for half in range(2):
            to = half * 2 + TILE_CORE[j]
            dest = {"dom": d if j < 2 else dom_at(-OFFSETS[j - 2]), "rep": to}
            slot = TILE_SLOT[j]
            cf = pltpu.make_async_remote_copy(gfeat.at[j, half], rf.at[slot, r], sem_sf.at[j, half],
                                              sem_rf.at[slot, r], device_id=dest, device_id_type=MESH)
            cs = pltpu.make_async_remote_copy(side.at[j], rs.at[slot, r], sem_ss.at[j, half],
                                              sem_rs.at[slot, r], device_id=dest, device_id_type=MESH)
            sends.append((j, to, cf, cs))
            if j < 2:
                @pl.when(r != to)
                def _():
                    cf.start()
                    cs.start()
            else:
                cf.start()
                cs.start()

    def mix_copy(i):
        to = lax.rem(d + i, n_dom)
        return pltpu.make_async_remote_copy(mix.at[to], rm.at[d], sem_sm.at[i], sem_rm.at[d],
                                            device_id={"dom": to, "rep": r}, device_id_type=MESH)

    def mix_start(i, _):
        mix_copy(i).start()
        return 0

    lax.fori_loop(1, n_dom, mix_start, 0)

    def take(dst, ss, rsem):
        pltpu.make_async_remote_copy(dst, dst, ss, rsem, device_id={"dom": d, "rep": peers[0]},
                                     device_id_type=MESH).wait_recv()

    feat_self = gfeat[c, y].astype(F32)
    side_self = side[c]
    for q in peers:
        take(rf.at[0, q], sem_sf.at[0, 0], sem_rf.at[0, q])
        take(rs.at[0, q], sem_ss.at[0, 0], sem_rs.at[0, q])
        feat_self = feat_self + rf[0, q].astype(F32)
        side_self = side_self + rs[0, q]
    is_low = c == 0
    zero = jnp.zeros_like(feat_self)
    total = jnp.concatenate([jnp.where(is_low, feat_self, zero), jnp.where(is_low, zero, feat_self)], axis=0)
    zside = jnp.zeros_like(side_self)
    total_side = jnp.concatenate([jnp.where(is_low, side_self, zside), jnp.where(is_low, zside, side_self)],
                                 axis=1)
    atoms = out_feat.shape[0]
    iota = lax.broadcasted_iota(jnp.int32, (atoms, TILE), 0)
    for q in range(2):
        hot = (iota == rows[pl.ds(2 * c + q, 1), :]).astype(F32).astype(BF16)
        slot = 1 + q
        got = None
        for s in range(n_rep):
            take(rf.at[slot, s], sem_sf.at[0, 0], sem_rf.at[slot, s])
            take(rs.at[slot, s], sem_ss.at[0, 0], sem_rs.at[slot, s])
            total = total + mm(hot, rf[slot, s])
            got = rs[slot, s] if got is None else got + rs[slot, s]
        for v in split3(got):
            total_side = total_side + nt(v, hot)
    part[r] = total.astype(BF16)
    pside[...] = total_side
    phase = []
    for i, q in enumerate(peers):
        cp = pltpu.make_async_remote_copy(part.at[r], part.at[r], sem_sp.at[i], sem_rp.at[r],
                                          device_id={"dom": d, "rep": q}, device_id_type=MESH)
        cp.start()
        phase.append(cp)
    cq = pltpu.make_async_remote_copy(pside, qside, sem_sq, sem_rq,
                                      device_id={"dom": d, "rep": r + 1 - 2 * c}, device_id_type=MESH)
    cq.start()

    def mix_add(i, value):
        frm = lax.rem(d + i, n_dom)
        take(rm.at[frm], sem_sm.at[0], sem_rm.at[frm])
        return value + rm[frm]

    out_mix[...] = lax.fori_loop(1, n_dom, mix_add, mix[d])
    cq.wait_recv()
    final = total_side + qside[...]
    out_force[...] = final[0:3]
    out_virial[...] = final[8:14]
    for q in peers:
        take(part.at[q], sem_sp.at[0], sem_rp.at[q])
    for half in range(2):
        out_feat[:, half * TILE:(half + 1) * TILE] = (
            part[2 * half].astype(F32) + part[2 * half + 1].astype(F32)).astype(BF16)
    for j, to, cf, cs in sends:
        if j < 2:
            @pl.when(r != to)
            def _():
                cf.wait_send()
                cs.wait_send()
        else:
            cf.wait_send()
            cs.wait_send()

    def mix_done(i, _):
        mix_copy(i).wait_send()
        return 0

    lax.fori_loop(1, n_dom, mix_done, 0)
    for cp in phase:
        cp.wait_send()
    cq.wait_send()


def on_device(n_dom, n_rep, features, positions, radial, mixing, readout, decay, send_rows, pair_home,
              pair_other, pair_kind, pair_image):
    atoms, channels = features.shape
    own = atoms // TILE
    n_ext = own + len(OFFSETS)
    kinds = radial.shape[0]
    dma = pltpu.SemaphoreType.DMA
    share = atoms // n_rep

    def params(cid=None):
        if cid is None:
            return pltpu.CompilerParams(vmem_limit_bytes=40 << 20)
        return pltpu.CompilerParams(collective_id=cid, has_side_effects=True, vmem_limit_bytes=40 << 20)

    def shape(dims, dtype):
        return jax.ShapeDtypeStruct(dims, dtype)

    mapped, tiles = pl.pallas_call(
        functools.partial(halo_kernel, n_dom),
        out_shape=(shape((n_ext, kinds, TILE, channels), BF16), shape((n_ext, 3, TILE), F32)),
        in_specs=[VMEM] * 4,
        out_specs=(VMEM, VMEM),
        scratch_shapes=[
            pltpu.VMEM((4, TILE, channels), BF16), pltpu.VMEM((4, 3, TILE), F32),
            pltpu.VMEM((4, TILE, channels), BF16), pltpu.VMEM((4, 3, TILE), F32),
            dma((4,)), dma((4,)), dma((4,)), dma((4,)),
        ],
        compiler_params=params(0),
        name="halo",
    )(features, positions, send_rows, radial)

    message = pl.pallas_call(
        forward_kernel,
        out_shape=shape((n_rep, share, channels), BF16),
        in_specs=[SMEM] * 5 + [VMEM] * 2,
        out_specs=VMEM,
        scratch_shapes=[pltpu.VMEM((2, 3, TILE, TILE), F32), pltpu.VMEM((own, TILE, channels), F32)],
        compiler_params=params(),
        name="forward_pairs",
    )(decay, pair_home, pair_other, pair_kind, pair_image, tiles, mapped)

    packed, slope, adjoint = pl.pallas_call(
        functools.partial(atom_kernel, n_rep),
        out_shape=(shape((atoms, channels), BF16), shape((atoms, channels), BF16),
                   shape((own, TILE, channels), BF16)),
        in_specs=[VMEM] * 3,
        out_specs=(VMEM,) * 3,
        scratch_shapes=[pltpu.VMEM((n_rep, share, channels), BF16)] * 3
        + [dma((n_rep,)) for _ in range(6)],
        compiler_params=params(1),
        name="atoms",
    )(message, mixing, readout.reshape(1, channels))

    gfeat, side, mix = pl.pallas_call(
        functools.partial(backward_kernel, n_rep),
        out_shape=(shape((n_ext, 2, TILE, channels // 2), BF16), shape((n_ext, 16, TILE), F32),
                   shape((n_dom, channels // n_dom, channels // n_rep), F32)),
        in_specs=[SMEM] * 5 + [VMEM] * 6,
        out_specs=(VMEM,) * 3,
        scratch_shapes=[
            pltpu.VMEM((n_ext, 3, TILE, TILE), F32), pltpu.VMEM((n_ext, 80, TILE), BF16),
            pltpu.VMEM((n_ext, 8, TILE), F32), pltpu.VMEM((n_ext, 8, TILE), F32),
            pltpu.VMEM((n_ext, TILE, channels), F32),
        ],
        compiler_params=params(),
        name="backward_pairs",
    )(decay, pair_home, pair_other, pair_kind, pair_image, tiles, mapped, adjoint, radial, packed, slope)

    mix_rows, mix_cols = channels // n_dom, channels // n_rep
    return pl.pallas_call(
        functools.partial(return_kernel, n_dom, n_rep),
        out_shape=(shape((atoms, channels), BF16), shape((3, atoms), F32), shape((6, atoms), F32),
                   shape((mix_rows, mix_cols), F32)),
        in_specs=[VMEM] * 4,
        out_specs=(VMEM,) * 4,
        scratch_shapes=[
            pltpu.VMEM((3, n_rep, TILE, channels // 2), BF16), pltpu.VMEM((3, n_rep, 16, TILE), F32),
            pltpu.VMEM((n_dom, mix_rows, mix_cols), F32), pltpu.VMEM((n_rep, atoms, channels // 2), BF16),
            pltpu.VMEM((16, atoms), F32), pltpu.VMEM((16, atoms), F32),
            dma((n_ext, 2)), dma((3, n_rep)), dma((n_ext, 2)), dma((3, n_rep)),
            dma((n_dom,)), dma((n_dom,)), dma((n_rep,)), dma((n_rep,)), dma, dma,
        ],
        compiler_params=params(2),
        name="return_gradients",
    )(gfeat, side, mix, send_rows)


def solution(mesh):
    in_specs = (
        P("dom", None),
        P(None, "dom"),
        P(),
        P(),
        P(),
        P(),
        P(None, "dom"),
        P(("dom", "rep")),
        P(("dom", "rep")),
        P(("dom", "rep")),
        P(None, ("dom", "rep")),
    )
    out_specs = (P("dom", None), P(None, "dom"), P(None, "dom"), P("dom", "rep"))
    body = functools.partial(on_device, mesh.shape["dom"], mesh.shape["rep"])
    return jax.shard_map(body, mesh=mesh, in_specs=in_specs, out_specs=out_specs, check_vma=False)
```

```python
import functools

import jax
import jax.numpy as jnp
from jax import lax
from jax.experimental import pallas as pl
from jax.experimental.pallas import tpu as pltpu
from jax.sharding import PartitionSpec as P

TILE = 128
OFFSETS = (1, -1, 2, -2)
CELL = 2.0
GROUP = 4
F32 = jnp.float32
BF16 = jnp.bfloat16
MESH = pl.DeviceIdType.MESH
VMEM = pl.BlockSpec(memory_space=pltpu.VMEM)
HBM = pl.BlockSpec(memory_space=pltpu.HBM)


def nt(a, b):
    return lax.dot_general(a, b, (((1,), (1,)), ((), ())), preferred_element_type=F32)


def tn(a, b):
    return lax.dot_general(a, b, (((0,), (0,)), ((), ())), preferred_element_type=F32)


def mm(a, b):
    return jnp.dot(a, b, preferred_element_type=F32)


def split3(x):
    hi = x.astype(BF16)
    rest = x - hi.astype(F32)
    mid = rest.astype(BF16)
    low = (rest - mid.astype(F32)).astype(BF16)
    return hi, mid, low


def front_kernel(n_dom, n_rep, feat_h, pos_h, rows_h, radial_h, mixing_h, readout_h, decay_h, home_h, other_h,
                 kind_h, image_h, mapped, tiles, kern_t, packed, slope, adjoint, radial,
                 feat, pos, rows, mixing, readout, decay, home, other, kind, image,
                 sendf, sendp, recvf, recvp, col, acc, msg, recv, pk, sl,
                 load, sf, sp, rf, rp, s1, r1, s2, r2, s3, r3):
    d = lax.axis_index("dom")
    r = lax.axis_index("rep")
    loads = [pltpu.make_async_copy(src, dst, load.at[i]) for i, (src, dst) in enumerate((
        (rows_h, rows), (feat_h, feat), (pos_h, pos), (radial_h, radial), (decay_h, decay), (home_h, home),
        (other_h, other), (kind_h, kind), (image_h, image), (mixing_h, mixing), (readout_h, readout)))]
    for copy in loads:
        copy.start()
    barrier = pltpu.get_barrier_semaphore()
    for o in OFFSETS:
        pl.semaphore_signal(barrier, inc=1, device_id={"dom": lax.rem(d + o + n_dom, n_dom), "rep": r},
                            device_id_type=MESH)
    peers = [lax.rem(r + i, n_rep) for i in range(1, n_rep)]
    for q in peers:
        pl.semaphore_signal(barrier, inc=1, device_id={"dom": d, "rep": q}, device_id_type=MESH)
    atoms = feat.shape[0]
    own = atoms // TILE
    iota = lax.broadcasted_iota(jnp.int32, (atoms, TILE), 0)
    for copy in loads[:3]:
        copy.wait()
    copies = []
    for t, o in enumerate(OFFSETS):
        hot = (iota == rows[t:t + 1, :]).astype(F32)
        sendf[t] = tn(hot.astype(BF16), feat[...]).astype(BF16)
        sendp[t] = jnp.dot(pos[...], hot, precision=lax.Precision.HIGHEST, preferred_element_type=F32)
        if t == 0:
            pl.semaphore_wait(barrier, 4 + n_rep - 1)
        to = {"dom": lax.rem(d + o + n_dom, n_dom), "rep": r}
        cf = pltpu.make_async_remote_copy(sendf.at[t], recvf.at[t], sf.at[t], rf.at[t],
                                          device_id=to, device_id_type=MESH)
        cp = pltpu.make_async_remote_copy(sendp.at[t], recvp.at[t], sp.at[t], rp.at[t],
                                          device_id=to, device_id_type=MESH)
        cf.start()
        cp.start()
        copies.append((cf, cp))

    def columns(j):
        for c in range(3):
            col[j, c] = jnp.transpose(jnp.broadcast_to(tiles[j][c:c + 1, :], (TILE, TILE)))

    for copy in loads[3:]:
        copy.wait()
    for j in range(own):
        tiles[j] = pos[:, j * TILE:(j + 1) * TILE]
        columns(j)

    def local(k, _):
        res = mm(feat[...], radial[k]).astype(BF16)
        for j in range(own):
            mapped[j, k] = res[j * TILE:(j + 1) * TILE]
        return 0

    lax.fori_loop(0, radial.shape[0], local, 0)
    for h in range(2):
        for t in (2 * h, 2 * h + 1):
            copies[t][0].wait_recv()
            copies[t][1].wait_recv()
            tiles[own + t] = recvp[t]
            columns(own + t)

        def distant(k, _):
            both = jnp.concatenate([recvf[2 * h], recvf[2 * h + 1]], axis=0)
            res = mm(both, radial[k]).astype(BF16)
            mapped[own + 2 * h, k] = res[:TILE]
            mapped[own + 2 * h + 1, k] = res[TILE:]
            return 0

        lax.fori_loop(0, radial.shape[0], distant, 0)

    acc[...] = jnp.zeros_like(acc)
    pairs = home.shape[0]

    def forward(g, _):
        left, right = [], []
        for u in range(GROUP):
            p = g * GROUP + u
            h, o, k = home[p], other[p], kind[p]
            row = tiles[o]
            d2 = None
            for c in range(3):
                sep = (row[c:c + 1, :] + image[c, p].astype(F32) * CELL) - col[h, c]
                d2 = sep * sep if d2 is None else d2 + sep * sep
            kern = jnp.exp(d2 * (-decay[k]))
            left.append(jnp.concatenate(
                [(kern * (h == i).astype(F32)).astype(BF16) for i in range(own)], axis=0))
            right.append(mapped[o, k])
        acc[...] += mm(jnp.concatenate(left, axis=1), jnp.concatenate(right, axis=0))
        return 0

    lax.fori_loop(0, pairs // GROUP, forward, 0)
    share = atoms // n_rep
    for q in range(n_rep):
        msg[q] = acc[q * share:(q + 1) * share, :].astype(BF16)

    def push(src, dst, ss, rs, q):
        copy = pltpu.make_async_remote_copy(src, dst, ss, rs, device_id={"dom": d, "rep": q},
                                            device_id_type=MESH)
        copy.start()
        return copy

    def take(dst, ss, rs, q):
        pltpu.make_async_remote_copy(dst, dst, ss, rs, device_id={"dom": d, "rep": q},
                                     device_id_type=MESH).wait_recv()

    def transposed(g, _):
        for u in range(GROUP):
            p = g * GROUP + u
            h, o, k = home[p], other[p], kind[p]
            row = tiles[h]
            d2 = None
            for c in range(3):
                sep = col[o, c] - (row[c:c + 1, :] - image[c, p].astype(F32) * CELL)
                d2 = sep * sep if d2 is None else d2 + sep * sep
            kern_t[p] = jnp.exp(d2 * (-decay[k]))
        return 0

    sent = [push(msg.at[q], recv.at[r], s1.at[i], r1.at[r], q) for i, q in enumerate(peers)]
    half = pairs // GROUP // 2
    lax.fori_loop(0, half, transposed, 0)
    total = msg[r].astype(F32)
    for i, q in enumerate(peers):
        take(recv.at[q], s1.at[i], r1.at[q], q)
        total = total + recv[q].astype(F32)
    low = total.astype(BF16)
    pk[r] = low
    mixed = mm(low, mixing[...])
    sig = jax.nn.sigmoid(mixed)
    sl[r] = (readout[...] * sig * (1.0 + mixed * (1.0 - sig))).astype(BF16)
    sent += [push(sl.at[r], sl.at[r], s3.at[i], r3.at[r], q) for i, q in enumerate(peers)]
    sent += [push(pk.at[r], pk.at[r], s2.at[i], r2.at[r], q) for i, q in enumerate(peers)]
    lax.fori_loop(half, pairs // GROUP, transposed, 0)
    for i, q in enumerate(peers):
        take(sl.at[q], s3.at[i], r3.at[q], q)
    full = sl[...].reshape(-1, mixing.shape[0])
    slope[...] = full
    adj = nt(full, mixing[...]).astype(BF16)
    for j in range(own):
        adjoint[j] = adj[j * TILE:(j + 1) * TILE]
    for i, q in enumerate(peers):
        take(pk.at[q], s2.at[i], r2.at[q], q)
    packed[...] = pk[...].reshape(-1, mixing.shape[0])
    for cf, cp in copies:
        cf.wait_send()
        cp.wait_send()
    for copy in sent:
        copy.wait_send()


def backward_kernel(n_rep, decay_h, home_h, other_h, kind_h, image_h, tiles, mapped, kern_t, adjoint, radial,
                    packed, slope, gfeat, side, mix, decay, home, other, kind, image, moments, first, second,
                    acc, load):
    loads = [pltpu.make_async_copy(src, dst, load.at[i]) for i, (src, dst) in enumerate((
        (decay_h, decay), (home_h, home), (other_h, other), (kind_h, kind), (image_h, image)))]
    for copy in loads:
        copy.start()
    n_ext = tiles.shape[0]
    for j in range(n_ext):
        pos = tiles[j]
        x, y, z = pos[0:1, :], pos[1:2, :], pos[2:3, :]
        zero = jnp.zeros((2, TILE), F32)
        one_rows = jnp.concatenate([x, y, z, x, x, y, zero], axis=0)
        two_rows = jnp.concatenate([x, y, z, y, z, z, zero], axis=0)
        first[j] = one_rows
        second[j] = two_rows
        stack = jnp.concatenate([one_rows * two_rows, one_rows, two_rows], axis=0)
        parts = [v.astype(F32) for v in split3(stack)]
        moments[j] = jnp.concatenate(
            [parts[0], jnp.ones((8, TILE), F32), parts[1], parts[2]], axis=0).astype(BF16)
    acc[...] = jnp.zeros_like(acc)
    side[...] = jnp.zeros_like(side)
    sub = lax.broadcasted_iota(jnp.int32, (8, TILE), 0)

    def rows_of(a, b):
        return ((sub == a[0]) | (sub == a[1]) | (sub == a[2])), ((sub == b[0]) | (sub == b[1]))

    is_x1, is_y1 = rows_of((0, 3, 4), (1, 5))
    is_x2, is_y2 = (sub == 0), ((sub == 1) | (sub == 3))

    def fold(res):
        quad = res[0:8] + res[32:40] + res[56:64]
        lin1 = res[8:16] + res[40:48] + res[64:72]
        lin2 = res[16:24] + res[48:56] + res[72:80]
        return quad, lin1, lin2, res[24:32]

    def combine(res, a, b):
        quad, lin1, lin2, one = fold(res)
        force = lin1 - a * one
        virial = -0.5 * (quad - a * lin2 - b * lin1 + a * b * one)
        return jnp.concatenate([force, virial], axis=0)

    for copy in loads:
        copy.wait()

    def body(g, _):
        found = []
        for u in range(GROUP):
            p = g * GROUP + u
            h, o, k = home[p], other[p], kind[p]
            rate = decay[k]
            shift = [image[c, p].astype(F32) * CELL for c in range(3)]
            kern = kern_t[p]
            adj = adjoint[h]
            weight = (-2.0 * rate) * kern * nt(mapped[o, k], adj)
            back = mm(kern.astype(BF16), adj).astype(BF16)
            part = nt(back, radial[k])
            hi = weight.astype(BF16)
            lo = (weight - hi.astype(F32)).astype(BF16)
            near_res = mm(moments[o], hi) + mm(moments[o], lo)
            far_res = nt(moments[h], hi) + nt(moments[h], lo)
            s1 = jnp.where(is_x1, shift[0], jnp.where(is_y1, shift[1], shift[2]))
            s2 = jnp.where(is_x2, shift[0], jnp.where(is_y2, shift[1], shift[2]))
            near_side = combine(near_res, first[h] - s1, second[h] - s2)
            far_side = combine(far_res, first[o] + s1, second[o] + s2)
            found.append((h, o, part, near_side, far_side))
        for h, o, part, near_side, far_side in found:
            acc[o] += part
            side[h] += near_side
            side[o] += far_side
        return 0

    lax.fori_loop(0, home.shape[0] // GROUP, body, 0)
    for j in range(n_ext):
        for half in range(2):
            gfeat[j, half] = acc[j, :, half * TILE:(half + 1) * TILE].astype(BF16)
    r = lax.axis_index("rep")
    channels = slope.shape[1]
    share = channels // n_rep
    pick = (lax.broadcasted_iota(jnp.int32, (channels, share), 0)
            == lax.broadcasted_iota(jnp.int32, (channels, share), 1) + r * share).astype(BF16)
    cols = mm(slope[...], pick).astype(BF16)
    res = tn(packed[...], cols)
    mix[...] = res.reshape(mix.shape)


TILE_CORE = (0, 1, 0, 0, 1, 1)
TILE_SLOT = (0, 0, 1, 2, 1, 2)


def return_kernel(n_dom, n_rep, gfeat, side, mix, rows, out_feat, out_force, out_virial, out_mix,
                  rf, rs, rm, part, pside, qside,
                  sem_sf, sem_rf, sem_ss, sem_rs, sem_sm, sem_rm, sem_sp, sem_rp, sem_sq, sem_rq):
    d = lax.axis_index("dom")
    r = lax.axis_index("rep")
    y = lax.div(r, 2)
    c = lax.rem(r, 2)

    def dom_at(o):
        return lax.rem(d + o + n_dom, n_dom)

    barrier = pltpu.get_barrier_semaphore()

    def hello(dom, rep):
        pl.semaphore_signal(barrier, inc=1, device_id={"dom": dom, "rep": rep}, device_id_type=MESH)

    mine = [(c + 1), -(c + 1)]
    peers = [lax.rem(r + i, n_rep) for i in range(1, n_rep)]
    for o in mine:
        for q in range(n_rep):
            hello(dom_at(o), q)
    for q in peers:
        hello(d, q)

    def greet(i, _):
        hello(lax.rem(d + i, n_dom), r)
        return 0

    lax.fori_loop(1, n_dom, greet, 0)
    pl.semaphore_wait(barrier, 2 * n_rep + n_rep - 1 + n_dom - 1)

    sends = []
    for j in (2, 3, 4, 5, 0, 1):
        for half in range(2):
            to = half * 2 + TILE_CORE[j]
            dest = {"dom": d if j < 2 else dom_at(-OFFSETS[j - 2]), "rep": to}
            slot = TILE_SLOT[j]
            cf = pltpu.make_async_remote_copy(gfeat.at[j, half], rf.at[slot, r], sem_sf.at[j, half],
                                              sem_rf.at[slot, r], device_id=dest, device_id_type=MESH)
            cs = pltpu.make_async_remote_copy(side.at[j], rs.at[slot, r], sem_ss.at[j, half],
                                              sem_rs.at[slot, r], device_id=dest, device_id_type=MESH)
            sends.append((j, to, cf, cs))
            if j < 2:
                @pl.when(r != to)
                def _():
                    cf.start()
                    cs.start()
            else:
                cf.start()
                cs.start()

    def mix_copy(i):
        to = lax.rem(d + i, n_dom)
        return pltpu.make_async_remote_copy(mix.at[to], rm.at[d], sem_sm.at[i], sem_rm.at[d],
                                            device_id={"dom": to, "rep": r}, device_id_type=MESH)

    def mix_start(i, _):
        mix_copy(i).start()
        return 0

    lax.fori_loop(1, n_dom, mix_start, 0)

    def take(dst, ss, rsem):
        pltpu.make_async_remote_copy(dst, dst, ss, rsem, device_id={"dom": d, "rep": peers[0]},
                                     device_id_type=MESH).wait_recv()

    feat_self = gfeat[c, y].astype(F32)
    side_self = side[c]
    for q in peers:
        take(rf.at[0, q], sem_sf.at[0, 0], sem_rf.at[0, q])
        take(rs.at[0, q], sem_ss.at[0, 0], sem_rs.at[0, q])
        feat_self = feat_self + rf[0, q].astype(F32)
        side_self = side_self + rs[0, q]
    is_low = c == 0
    zero = jnp.zeros_like(feat_self)
    total = jnp.concatenate([jnp.where(is_low, feat_self, zero), jnp.where(is_low, zero, feat_self)], axis=0)
    zside = jnp.zeros_like(side_self)
    total_side = jnp.concatenate([jnp.where(is_low, side_self, zside), jnp.where(is_low, zside, side_self)],
                                 axis=1)
    atoms = out_feat.shape[0]
    iota = lax.broadcasted_iota(jnp.int32, (atoms, TILE), 0)
    for q in range(2):
        hot = (iota == rows[pl.ds(2 * c + q, 1), :]).astype(F32).astype(BF16)
        slot = 1 + q
        got = None
        for s in range(n_rep):
            take(rf.at[slot, s], sem_sf.at[0, 0], sem_rf.at[slot, s])
            take(rs.at[slot, s], sem_ss.at[0, 0], sem_rs.at[slot, s])
            total = total + mm(hot, rf[slot, s])
            got = rs[slot, s] if got is None else got + rs[slot, s]
        for v in split3(got):
            total_side = total_side + nt(v, hot)
    part[r] = total.astype(BF16)
    pside[...] = total_side
    phase = []
    for i, q in enumerate(peers):
        cp = pltpu.make_async_remote_copy(part.at[r], part.at[r], sem_sp.at[i], sem_rp.at[r],
                                          device_id={"dom": d, "rep": q}, device_id_type=MESH)
        cp.start()
        phase.append(cp)
    cq = pltpu.make_async_remote_copy(pside, qside, sem_sq, sem_rq,
                                      device_id={"dom": d, "rep": r + 1 - 2 * c}, device_id_type=MESH)
    cq.start()

    def mix_add(i, value):
        frm = lax.rem(d + i, n_dom)
        take(rm.at[frm], sem_sm.at[0], sem_rm.at[frm])
        return value + rm[frm]

    out_mix[...] = lax.fori_loop(1, n_dom, mix_add, mix[d])
    cq.wait_recv()
    final = total_side + qside[...]
    out_force[...] = final[0:3]
    out_virial[...] = final[8:14]
    for q in peers:
        take(part.at[q], sem_sp.at[0], sem_rp.at[q])
    for half in range(2):
        out_feat[:, half * TILE:(half + 1) * TILE] = (
            part[2 * half].astype(F32) + part[2 * half + 1].astype(F32)).astype(BF16)
    for j, to, cf, cs in sends:
        if j < 2:
            @pl.when(r != to)
            def _():
                cf.wait_send()
                cs.wait_send()
        else:
            cf.wait_send()
            cs.wait_send()

    def mix_done(i, _):
        mix_copy(i).wait_send()
        return 0

    lax.fori_loop(1, n_dom, mix_done, 0)
    for cp in phase:
        cp.wait_send()
    cq.wait_send()


def copy_out(a, b, c, d, a_h, b_h, c_h, d_h, sem):
    copies = [pltpu.make_async_copy(src, dst, sem.at[i])
              for i, (src, dst) in enumerate(((a, a_h), (b, b_h), (c, c_h), (d, d_h)))]
    for copy in copies:
        copy.start()
    for copy in copies:
        copy.wait()


def on_device(n_dom, n_rep, features, positions, radial, mixing, readout, decay, send_rows, pair_home,
              pair_other, pair_kind, pair_image):
    atoms, channels = features.shape
    own = atoms // TILE
    n_ext = own + len(OFFSETS)
    kinds = radial.shape[0]
    dma = pltpu.SemaphoreType.DMA
    share = atoms // n_rep

    def params(cid=None):
        if cid is None:
            return pltpu.CompilerParams(vmem_limit_bytes=40 << 20)
        return pltpu.CompilerParams(collective_id=cid, has_side_effects=True, vmem_limit_bytes=40 << 20)

    def shape(dims, dtype):
        return jax.ShapeDtypeStruct(dims, dtype)

    def pair_tables():
        return [pltpu.SMEM(decay.shape, F32)] + [
            pltpu.SMEM(a.shape, jnp.int32) for a in (pair_home, pair_other, pair_kind, pair_image)]

    readout_row = readout.reshape(1, channels)
    mapped, tiles, kern_t, packed, slope, adjoint, radial_near = pl.pallas_call(
        functools.partial(front_kernel, n_dom, n_rep),
        out_shape=(shape((n_ext, kinds, TILE, channels), BF16), shape((n_ext, 3, TILE), F32),
                   shape((pair_home.shape[0], TILE, TILE), F32), shape((atoms, channels), BF16),
                   shape((atoms, channels), BF16), shape((own, TILE, channels), BF16),
                   shape(radial.shape, BF16)),
        in_specs=[HBM] * 11,
        out_specs=(VMEM,) * 7,
        scratch_shapes=[
            pltpu.VMEM(features.shape, BF16), pltpu.VMEM(positions.shape, F32),
            pltpu.VMEM(send_rows.shape, jnp.int32),
            pltpu.VMEM(mixing.shape, BF16), pltpu.VMEM(readout_row.shape, F32), *pair_tables(),
            pltpu.VMEM((4, TILE, channels), BF16), pltpu.VMEM((4, 3, TILE), F32),
            pltpu.VMEM((4, TILE, channels), BF16), pltpu.VMEM((4, 3, TILE), F32),
            pltpu.VMEM((n_ext, 3, TILE, TILE), F32), pltpu.VMEM((atoms, channels), F32),
            *[pltpu.VMEM((n_rep, share, channels), BF16)] * 4,
            dma((11,)), dma((4,)), dma((4,)), dma((4,)), dma((4,)), *[dma((n_rep,)) for _ in range(6)],
        ],
        compiler_params=params(0),
        name="front",
    )(*[pltpu.with_memory_space_constraint(a, pltpu.HBM) for a in (
        features, positions, send_rows, radial, mixing, readout_row, decay, pair_home, pair_other, pair_kind,
        pair_image)])

    gfeat, side, mix = pl.pallas_call(
        functools.partial(backward_kernel, n_rep),
        out_shape=(shape((n_ext, 2, TILE, channels // 2), BF16), shape((n_ext, 16, TILE), F32),
                   shape((n_dom, channels // n_dom, channels // n_rep), F32)),
        in_specs=[HBM] * 5 + [VMEM] * 7,
        out_specs=(VMEM,) * 3,
        scratch_shapes=[
            *pair_tables(), pltpu.VMEM((n_ext, 80, TILE), BF16),
            pltpu.VMEM((n_ext, 8, TILE), F32), pltpu.VMEM((n_ext, 8, TILE), F32),
            pltpu.VMEM((n_ext, TILE, channels), F32), dma((5,)),
        ],
        compiler_params=params(),
        name="backward_pairs",
    )(*[pltpu.with_memory_space_constraint(a, pltpu.HBM) for a in (
        decay, pair_home, pair_other, pair_kind, pair_image)],
      tiles, mapped, kern_t, adjoint, radial_near, packed, slope)

    mix_rows, mix_cols = channels // n_dom, channels // n_rep
    results = pl.pallas_call(
        functools.partial(return_kernel, n_dom, n_rep),
        out_shape=(shape((atoms, channels), BF16), shape((3, atoms), F32), shape((6, atoms), F32),
                   shape((mix_rows, mix_cols), F32)),
        in_specs=[VMEM] * 4,
        out_specs=(VMEM,) * 4,
        scratch_shapes=[
            pltpu.VMEM((3, n_rep, TILE, channels // 2), BF16), pltpu.VMEM((3, n_rep, 16, TILE), F32),
            pltpu.VMEM((n_dom, mix_rows, mix_cols), F32), pltpu.VMEM((n_rep, atoms, channels // 2), BF16),
            pltpu.VMEM((16, atoms), F32), pltpu.VMEM((16, atoms), F32),
            dma((n_ext, 2)), dma((3, n_rep)), dma((n_ext, 2)), dma((3, n_rep)),
            dma((n_dom,)), dma((n_dom,)), dma((n_rep,)), dma((n_rep,)), dma, dma,
        ],
        compiler_params=params(2),
        name="return_gradients",
    )(gfeat, side, mix, send_rows)
    return pl.pallas_call(
        copy_out,
        out_shape=tuple(shape(a.shape, a.dtype) for a in results),
        in_specs=[VMEM] * 4,
        out_specs=(HBM,) * 4,
        scratch_shapes=[dma((4,))],
        compiler_params=pltpu.CompilerParams(vmem_limit_bytes=4 << 20),
        name="copy_out",
    )(*results)


def solution(mesh):
    in_specs = (
        P("dom", None),
        P(None, "dom"),
        P(),
        P(),
        P(),
        P(),
        P(None, "dom"),
        P(("dom", "rep")),
        P(("dom", "rep")),
        P(("dom", "rep")),
        P(None, ("dom", "rep")),
    )
    out_specs = (P("dom", None), P(None, "dom"), P(None, "dom"), P("dom", "rep"))
    body = functools.partial(on_device, mesh.shape["dom"], mesh.shape["rep"])
    return jax.shard_map(body, mesh=mesh, in_specs=in_specs, out_specs=out_specs, check_vma=False)
```

```python
import functools

import jax
import jax.numpy as jnp
from jax import lax
from jax.experimental import pallas as pl
from jax.experimental.pallas import tpu as pltpu
from jax.sharding import PartitionSpec as P

TILE = 128
OFFSETS = (1, -1, 2, -2)
CELL = 2.0
GROUP = 4
BACK_GROUP = 8
F32 = jnp.float32
BF16 = jnp.bfloat16
MESH = pl.DeviceIdType.MESH
VMEM = pl.BlockSpec(memory_space=pltpu.VMEM)
HBM = pl.BlockSpec(memory_space=pltpu.HBM)


def nt(a, b):
    return lax.dot_general(a, b, (((1,), (1,)), ((), ())), preferred_element_type=F32)


def tn(a, b):
    return lax.dot_general(a, b, (((0,), (0,)), ((), ())), preferred_element_type=F32)


def mm(a, b):
    return jnp.dot(a, b, preferred_element_type=F32)


def split3(x):
    hi = x.astype(BF16)
    rest = x - hi.astype(F32)
    mid = rest.astype(BF16)
    low = (rest - mid.astype(F32)).astype(BF16)
    return hi, mid, low


def front_kernel(n_dom, n_rep, feat_h, pos_h, rows_h, radial_h, mixing_h, readout_h, decay_h, home_h, other_h,
                 kind_h, image_h, mapped, tiles, kern_t, packed, slope, adjoint, radial,
                 feat, pos, rows, mixing, readout, decay, home, other, kind, image,
                 sendf, sendp, recvf, recvp, col, acc, msg, recv, pk, sl,
                 load, sf, sp, rf, rp, s4, r4, s5, r5, s1, r1, s2, r2, s3, r3):
    d = lax.axis_index("dom")
    r = lax.axis_index("rep")
    loads = [pltpu.make_async_copy(src, dst, load.at[i]) for i, (src, dst) in enumerate((
        (rows_h, rows), (feat_h, feat), (pos_h, pos), (radial_h, radial), (decay_h, decay), (home_h, home),
        (other_h, other), (kind_h, kind), (image_h, image), (mixing_h, mixing), (readout_h, readout)))]
    for copy in loads:
        copy.start()
    barrier = pltpu.get_barrier_semaphore()
    c = lax.rem(r, 2)
    partner = {"dom": d, "rep": r + 1 - 2 * c}
    steps = (c + 1, -(c + 1))
    for o in steps:
        pl.semaphore_signal(barrier, inc=1, device_id={"dom": lax.rem(d + o + n_dom, n_dom), "rep": r},
                            device_id_type=MESH)
    peers = [lax.rem(r + i, n_rep) for i in range(1, n_rep)]
    for q in peers:
        pl.semaphore_signal(barrier, inc=1, device_id={"dom": d, "rep": q}, device_id_type=MESH)
    atoms = feat.shape[0]
    own = atoms // TILE
    iota = lax.broadcasted_iota(jnp.int32, (atoms, TILE), 0)
    for copy in loads[:3]:
        copy.wait()
    copies = []
    for q, o in enumerate(steps):
        t = 2 * c + q
        hot = (iota == rows[pl.ds(t, 1), :]).astype(F32)
        sendf[q] = tn(hot.astype(BF16), feat[...]).astype(BF16)
        sendp[q] = jnp.dot(pos[...], hot, precision=lax.Precision.HIGHEST, preferred_element_type=F32)
        if q == 0:
            pl.semaphore_wait(barrier, 2 + n_rep - 1)
        to = {"dom": lax.rem(d + o + n_dom, n_dom), "rep": r}
        cf = pltpu.make_async_remote_copy(sendf.at[q], recvf.at[t], sf.at[q], rf.at[t],
                                          device_id=to, device_id_type=MESH)
        cp = pltpu.make_async_remote_copy(sendp.at[q], recvp.at[t], sp.at[q], rp.at[t],
                                          device_id=to, device_id_type=MESH)
        cf.start()
        cp.start()
        copies += [cf, cp]

    def columns(j):
        for c in range(3):
            col[j, c] = jnp.transpose(jnp.broadcast_to(tiles[j][c:c + 1, :], (TILE, TILE)))

    for copy in loads[3:]:
        copy.wait()
    for j in range(own):
        tiles[j] = pos[:, j * TILE:(j + 1) * TILE]
        columns(j)

    def local(k, _):
        res = mm(feat[...], radial[k]).astype(BF16)
        for j in range(own):
            mapped[j, k] = res[j * TILE:(j + 1) * TILE]
        return 0

    lax.fori_loop(0, radial.shape[0], local, 0)
    def distant(base, k):
        both = recvf[pl.ds(base, 2)].reshape(2 * TILE, -1)
        res = mm(both, radial[k]).astype(BF16)
        mapped[own + base, k] = res[:TILE]
        mapped[own + base + 1, k] = res[TILE:]

    def unpack(base):
        for q in range(2):
            tiles[own + base + q] = recvp[base + q]
            columns(own + base + q)
        lax.fori_loop(0, radial.shape[0], lambda k, _: (distant(base, k), 0)[1], 0)

    relays = []
    for q in range(2):
        t = 2 * c + q
        copies[2 * q].wait_recv()
        copies[2 * q + 1].wait_recv()
        relays.append(pltpu.make_async_remote_copy(recvf.at[t], recvf.at[t], s4.at[q], r4.at[t],
                                                   device_id=partner, device_id_type=MESH))
        relays.append(pltpu.make_async_remote_copy(recvp.at[t], recvp.at[t], s5.at[q], r5.at[t],
                                                   device_id=partner, device_id_type=MESH))
        relays[-2].start()
        relays[-1].start()
    unpack(2 * c)
    for q in range(2):
        t = 2 * (1 - c) + q
        for dst, ss, rs in ((recvf.at[t], s4.at[q], r4.at[t]), (recvp.at[t], s5.at[q], r5.at[t])):
            pltpu.make_async_remote_copy(dst, dst, ss, rs, device_id=partner, device_id_type=MESH).wait_recv()
    unpack(2 * (1 - c))

    acc[...] = jnp.zeros_like(acc)
    pairs = home.shape[0]

    def forward(g, _):
        left, right = [], []
        for u in range(GROUP):
            p = g * GROUP + u
            h, o, k = home[p], other[p], kind[p]
            row = tiles[o]
            d2 = None
            for c in range(3):
                sep = (row[c:c + 1, :] + image[c, p].astype(F32) * CELL) - col[h, c]
                d2 = sep * sep if d2 is None else d2 + sep * sep
            kern = jnp.exp(d2 * (-decay[k]))
            left.append(jnp.concatenate(
                [(kern * (h == i).astype(F32)).astype(BF16) for i in range(own)], axis=0))
            right.append(mapped[o, k])
        acc[...] += mm(jnp.concatenate(left, axis=1), jnp.concatenate(right, axis=0))
        return 0

    lax.fori_loop(0, pairs // GROUP, forward, 0)
    share = atoms // n_rep
    for q in range(n_rep):
        msg[q] = acc[q * share:(q + 1) * share, :].astype(BF16)

    def push(src, dst, ss, rs, q):
        copy = pltpu.make_async_remote_copy(src, dst, ss, rs, device_id={"dom": d, "rep": q},
                                            device_id_type=MESH)
        copy.start()
        return copy

    def take(dst, ss, rs, q):
        pltpu.make_async_remote_copy(dst, dst, ss, rs, device_id={"dom": d, "rep": q},
                                     device_id_type=MESH).wait_recv()

    def transposed(g, _):
        for u in range(GROUP):
            p = g * GROUP + u
            h, o, k = home[p], other[p], kind[p]
            row = tiles[h]
            d2 = None
            for c in range(3):
                sep = col[o, c] - (row[c:c + 1, :] - image[c, p].astype(F32) * CELL)
                d2 = sep * sep if d2 is None else d2 + sep * sep
            kern_t[p] = jnp.exp(d2 * (-decay[k]))
        return 0

    sent = [push(msg.at[q], recv.at[r], s1.at[i], r1.at[r], q) for i, q in enumerate(peers)]
    half = pairs // GROUP // 2
    lax.fori_loop(0, half, transposed, 0)
    total = msg[r].astype(F32)
    for i, q in enumerate(peers):
        take(recv.at[q], s1.at[i], r1.at[q], q)
        total = total + recv[q].astype(F32)
    low = total.astype(BF16)
    pk[r] = low
    mixed = mm(low, mixing[...])
    sig = jax.nn.sigmoid(mixed)
    sl[r] = (readout[...] * sig * (1.0 + mixed * (1.0 - sig))).astype(BF16)
    sent += [push(sl.at[r], sl.at[r], s3.at[i], r3.at[r], q) for i, q in enumerate(peers)]
    sent += [push(pk.at[r], pk.at[r], s2.at[i], r2.at[r], q) for i, q in enumerate(peers)]
    lax.fori_loop(half, pairs // GROUP, transposed, 0)
    for i, q in enumerate(peers):
        take(sl.at[q], s3.at[i], r3.at[q], q)
    full = sl[...].reshape(-1, mixing.shape[0])
    slope[...] = full
    adj = nt(full, mixing[...]).astype(BF16)
    for j in range(own):
        adjoint[j] = adj[j * TILE:(j + 1) * TILE]
    for i, q in enumerate(peers):
        take(pk.at[q], s2.at[i], r2.at[q], q)
    packed[...] = pk[...].reshape(-1, mixing.shape[0])
    for copy in copies + relays + sent:
        copy.wait_send()


def backward_kernel(n_rep, decay_h, home_h, other_h, kind_h, image_h, tiles, mapped, kern_t, adjoint, radial,
                    packed, slope, gfeat, side, mix, decay, home, other, kind, image, moments, first, second,
                    acc, load):
    loads = [pltpu.make_async_copy(src, dst, load.at[i]) for i, (src, dst) in enumerate((
        (decay_h, decay), (home_h, home), (other_h, other), (kind_h, kind), (image_h, image)))]
    for copy in loads:
        copy.start()
    n_ext = tiles.shape[0]
    for j in range(n_ext):
        pos = tiles[j]
        x, y, z = pos[0:1, :], pos[1:2, :], pos[2:3, :]
        zero = jnp.zeros((2, TILE), F32)
        one_rows = jnp.concatenate([x, y, z, x, x, y, zero], axis=0)
        two_rows = jnp.concatenate([x, y, z, y, z, z, zero], axis=0)
        first[j] = one_rows
        second[j] = two_rows
        stack = jnp.concatenate([one_rows * two_rows, one_rows, two_rows], axis=0)
        parts = [v.astype(F32) for v in split3(stack)]
        table = jnp.concatenate(
            [parts[0], jnp.ones((8, TILE), F32), parts[1], parts[2]], axis=0).astype(BF16)
        moments[j] = jnp.concatenate([table, table], axis=1)
    acc[...] = jnp.zeros_like(acc)
    side[...] = jnp.zeros_like(side)
    sub = lax.broadcasted_iota(jnp.int32, (8, TILE), 0)

    def rows_of(a, b):
        return ((sub == a[0]) | (sub == a[1]) | (sub == a[2])), ((sub == b[0]) | (sub == b[1]))

    is_x1, is_y1 = rows_of((0, 3, 4), (1, 5))
    is_x2, is_y2 = (sub == 0), ((sub == 1) | (sub == 3))

    def fold(res):
        quad = res[0:8] + res[32:40] + res[56:64]
        lin1 = res[8:16] + res[40:48] + res[64:72]
        lin2 = res[16:24] + res[48:56] + res[72:80]
        return quad, lin1, lin2, res[24:32]

    def combine(res, a, b):
        quad, lin1, lin2, one = fold(res)
        force = lin1 - a * one
        virial = -0.5 * (quad - a * lin2 - b * lin1 + a * b * one)
        return jnp.concatenate([force, virial], axis=0)

    for copy in loads:
        copy.wait()

    def body(g, _):
        found = []
        names = []
        weights = []
        for u in range(BACK_GROUP):
            p = g * BACK_GROUP + u
            h, o, k = home[p], other[p], kind[p]
            names.append((p, h, o, k))
            kern = kern_t[p]
            weight = (-2.0 * decay[k]) * kern * nt(mapped[o, k], adjoint[h])
            hi = weight.astype(BF16)
            lo = (weight - hi.astype(F32)).astype(BF16)
            weights.append((hi, lo))
        for (p, h, o, k), (hi, lo) in zip(names, weights):
            back = mm(kern_t[p].astype(BF16), adjoint[h]).astype(BF16)
            part = nt(back, radial[k])
            shift = [image[c, p].astype(F32) * CELL for c in range(3)]
            near_res = mm(moments[o], jnp.concatenate([hi, lo], axis=0))
            far_res = nt(moments[h], jnp.concatenate([hi, lo], axis=1))
            s1 = jnp.where(is_x1, shift[0], jnp.where(is_y1, shift[1], shift[2]))
            s2 = jnp.where(is_x2, shift[0], jnp.where(is_y2, shift[1], shift[2]))
            near_side = combine(near_res, first[h] - s1, second[h] - s2)
            far_side = combine(far_res, first[o] + s1, second[o] + s2)
            found.append((h, o, part, near_side, far_side))
        for h, o, part, near_side, far_side in found:
            acc[o] += part
            side[h] += near_side
            side[o] += far_side
        return 0

    lax.fori_loop(0, home.shape[0] // BACK_GROUP, body, 0)
    for j in range(n_ext):
        for half in range(2):
            gfeat[j, half] = acc[j, :, half * TILE:(half + 1) * TILE].astype(BF16)
    r = lax.axis_index("rep")
    channels = slope.shape[1]
    share = channels // n_rep
    pick = (lax.broadcasted_iota(jnp.int32, (channels, share), 0)
            == lax.broadcasted_iota(jnp.int32, (channels, share), 1) + r * share).astype(BF16)
    cols = mm(slope[...], pick).astype(BF16)
    res = tn(packed[...], cols)
    mix[...] = res.reshape(mix.shape)


def return_kernel(n_dom, n_rep, gfeat, side, mix, rows, out_feat, out_force, out_virial, out_mix,
                  gp, gs, sb, ss, rf, rs, rm, part, pside, qside,
                  sem_gf, sem_hf, sem_gs, sem_hs, sem_sf, sem_rf, sem_ss, sem_rs, sem_sm, sem_rm, sem_sp, sem_rp, sem_sq, sem_rq):
    d = lax.axis_index("dom")
    r = lax.axis_index("rep")
    y = lax.div(r, 2)
    c = lax.rem(r, 2)

    def dom_at(o):
        return lax.rem(d + o + n_dom, n_dom)

    barrier = pltpu.get_barrier_semaphore()

    def hello(dom, rep):
        pl.semaphore_signal(barrier, inc=1, device_id={"dom": dom, "rep": rep}, device_id_type=MESH)

    mine = [(c + 1), -(c + 1)]
    peers = [lax.rem(r + i, n_rep) for i in range(1, n_rep)]
    for o in mine:
        for half in range(n_rep // 2):
            hello(dom_at(o), 2 * half + c)
    for q in peers:
        hello(d, q)

    def greet(i, _):
        hello(lax.rem(d + i, n_dom), r)
        return 0

    lax.fori_loop(1, n_dom, greet, 0)
    pl.semaphore_wait(barrier, n_rep + n_rep - 1 + n_dom - 1)

    partner = {"dom": d, "rep": r + 1 - 2 * c}
    mate = 1 - c
    sends = []
    swaps = []
    for slot, j in ((1, 2 + 2 * mate), (2, 3 + 2 * mate), (0, mate)):
        cf = pltpu.make_async_remote_copy(gfeat.at[j], gp.at[slot], sem_gf.at[slot], sem_hf.at[slot],
                                          device_id=partner, device_id_type=MESH)
        cs = pltpu.make_async_remote_copy(side.at[j], gs.at[slot], sem_gs.at[slot], sem_hs.at[slot],
                                          device_id=partner, device_id_type=MESH)
        cf.start()
        cs.start()
        swaps.append((cf, cs))
        sends += [cf, cs]
    for (cf, cs), (slot, j) in zip(swaps, ((1, 2 + 2 * c), (2, 3 + 2 * c), (0, c))):
        cf.wait_recv()
        cs.wait_recv()
        sb[slot] = (gfeat[j].astype(F32) + gp[slot].astype(F32)).astype(BF16)
        ss[slot] = side[j] + gs[slot]
        for half in ((0, 1) if slot else (1 - y,)):
            dest = {"dom": dom_at(-mine[slot - 1]) if slot else d, "rep": 2 * half + c}
            nf = pltpu.make_async_remote_copy(sb.at[slot, half], rf.at[slot, y], sem_sf.at[slot, half],
                                              sem_rf.at[slot, y], device_id=dest, device_id_type=MESH)
            ns = pltpu.make_async_remote_copy(ss.at[slot], rs.at[slot, y], sem_ss.at[slot, half],
                                              sem_rs.at[slot, y], device_id=dest, device_id_type=MESH)
            nf.start()
            ns.start()
            sends += [nf, ns]

    def mix_copy(i):
        to = lax.rem(d + i, n_dom)
        return pltpu.make_async_remote_copy(mix.at[to], rm.at[d], sem_sm.at[i], sem_rm.at[d],
                                            device_id={"dom": to, "rep": r}, device_id_type=MESH)

    def mix_start(i, _):
        mix_copy(i).start()
        return 0

    lax.fori_loop(1, n_dom, mix_start, 0)

    def take(dst, ss, rsem):
        pltpu.make_async_remote_copy(dst, dst, ss, rsem, device_id={"dom": d, "rep": peers[0]},
                                     device_id_type=MESH).wait_recv()

    take(rf.at[0, 1 - y], sem_sf.at[0, 0], sem_rf.at[0, 1 - y])
    take(rs.at[0, 1 - y], sem_ss.at[0, 0], sem_rs.at[0, 1 - y])
    feat_self = sb[0, y].astype(F32) + rf[0, 1 - y].astype(F32)
    side_self = ss[0] + rs[0, 1 - y]
    is_low = c == 0
    zero = jnp.zeros_like(feat_self)
    total = jnp.concatenate([jnp.where(is_low, feat_self, zero), jnp.where(is_low, zero, feat_self)], axis=0)
    zside = jnp.zeros_like(side_self)
    total_side = jnp.concatenate([jnp.where(is_low, side_self, zside), jnp.where(is_low, zside, side_self)],
                                 axis=1)
    atoms = out_feat.shape[0]
    iota = lax.broadcasted_iota(jnp.int32, (atoms, TILE), 0)
    for q in range(2):
        hot = (iota == rows[pl.ds(2 * c + q, 1), :]).astype(F32).astype(BF16)
        slot = 1 + q
        got = None
        for s in range(n_rep // 2):
            take(rf.at[slot, s], sem_sf.at[0, 0], sem_rf.at[slot, s])
            take(rs.at[slot, s], sem_ss.at[0, 0], sem_rs.at[slot, s])
            total = total + mm(hot, rf[slot, s])
            got = rs[slot, s] if got is None else got + rs[slot, s]
        for v in split3(got):
            total_side = total_side + nt(v, hot)
    part[r] = total.astype(BF16)
    pside[...] = total_side
    phase = []
    for i, q in enumerate(peers):
        cp = pltpu.make_async_remote_copy(part.at[r], part.at[r], sem_sp.at[i], sem_rp.at[r],
                                          device_id={"dom": d, "rep": q}, device_id_type=MESH)
        cp.start()
        phase.append(cp)
    cq = pltpu.make_async_remote_copy(pside, qside, sem_sq, sem_rq,
                                      device_id={"dom": d, "rep": r + 1 - 2 * c}, device_id_type=MESH)
    cq.start()

    def mix_add(i, value):
        frm = lax.rem(d + i, n_dom)
        take(rm.at[frm], sem_sm.at[0], sem_rm.at[frm])
        return value + rm[frm]

    out_mix[...] = lax.fori_loop(1, n_dom, mix_add, mix[d])
    cq.wait_recv()
    final = total_side + qside[...]
    out_force[...] = final[0:3]
    out_virial[...] = final[8:14]
    for q in peers:
        take(part.at[q], sem_sp.at[0], sem_rp.at[q])
    for half in range(2):
        out_feat[:, half * TILE:(half + 1) * TILE] = (
            part[2 * half].astype(F32) + part[2 * half + 1].astype(F32)).astype(BF16)
    for copy in sends:
        copy.wait_send()

    def mix_done(i, _):
        mix_copy(i).wait_send()
        return 0

    lax.fori_loop(1, n_dom, mix_done, 0)
    for cp in phase:
        cp.wait_send()
    cq.wait_send()


def copy_out(a, b, c, d, a_h, b_h, c_h, d_h, sem):
    copies = [pltpu.make_async_copy(src, dst, sem.at[i])
              for i, (src, dst) in enumerate(((a, a_h), (b, b_h), (c, c_h), (d, d_h)))]
    for copy in copies:
        copy.start()
    for copy in copies:
        copy.wait()


def on_device(n_dom, n_rep, features, positions, radial, mixing, readout, decay, send_rows, pair_home,
              pair_other, pair_kind, pair_image):
    atoms, channels = features.shape
    own = atoms // TILE
    n_ext = own + len(OFFSETS)
    kinds = radial.shape[0]
    dma = pltpu.SemaphoreType.DMA
    share = atoms // n_rep

    def params(cid=None):
        if cid is None:
            return pltpu.CompilerParams(vmem_limit_bytes=40 << 20)
        return pltpu.CompilerParams(collective_id=cid, has_side_effects=True, vmem_limit_bytes=40 << 20)

    def shape(dims, dtype):
        return jax.ShapeDtypeStruct(dims, dtype)

    def pair_tables():
        return [pltpu.SMEM(decay.shape, F32)] + [
            pltpu.SMEM(a.shape, jnp.int32) for a in (pair_home, pair_other, pair_kind, pair_image)]

    readout_row = readout.reshape(1, channels)
    mapped, tiles, kern_t, packed, slope, adjoint, radial_near = pl.pallas_call(
        functools.partial(front_kernel, n_dom, n_rep),
        out_shape=(shape((n_ext, kinds, TILE, channels), BF16), shape((n_ext, 3, TILE), F32),
                   shape((pair_home.shape[0], TILE, TILE), F32), shape((atoms, channels), BF16),
                   shape((atoms, channels), BF16), shape((own, TILE, channels), BF16),
                   shape(radial.shape, BF16)),
        in_specs=[HBM] * 11,
        out_specs=(VMEM,) * 7,
        scratch_shapes=[
            pltpu.VMEM(features.shape, BF16), pltpu.VMEM(positions.shape, F32),
            pltpu.VMEM(send_rows.shape, jnp.int32),
            pltpu.VMEM(mixing.shape, BF16), pltpu.VMEM(readout_row.shape, F32), *pair_tables(),
            pltpu.VMEM((2, TILE, channels), BF16), pltpu.VMEM((2, 3, TILE), F32),
            pltpu.VMEM((4, TILE, channels), BF16), pltpu.VMEM((4, 3, TILE), F32),
            pltpu.VMEM((n_ext, 3, TILE, TILE), F32), pltpu.VMEM((atoms, channels), F32),
            *[pltpu.VMEM((n_rep, share, channels), BF16)] * 4,
            dma((11,)), *[dma((4,)) for _ in range(8)], *[dma((n_rep,)) for _ in range(6)],
        ],
        compiler_params=params(0),
        name="front",
    )(*[pltpu.with_memory_space_constraint(a, pltpu.HBM) for a in (
        features, positions, send_rows, radial, mixing, readout_row, decay, pair_home, pair_other, pair_kind,
        pair_image)])

    gfeat, side, mix = pl.pallas_call(
        functools.partial(backward_kernel, n_rep),
        out_shape=(shape((n_ext, 2, TILE, channels // 2), BF16), shape((n_ext, 16, TILE), F32),
                   shape((n_dom, channels // n_dom, channels // n_rep), F32)),
        in_specs=[HBM] * 5 + [VMEM] * 7,
        out_specs=(VMEM,) * 3,
        scratch_shapes=[
            *pair_tables(), pltpu.VMEM((n_ext, 80, 2 * TILE), BF16),
            pltpu.VMEM((n_ext, 8, TILE), F32), pltpu.VMEM((n_ext, 8, TILE), F32),
            pltpu.VMEM((n_ext, TILE, channels), F32), dma((5,)),
        ],
        compiler_params=params(),
        name="backward_pairs",
    )(*[pltpu.with_memory_space_constraint(a, pltpu.HBM) for a in (
        decay, pair_home, pair_other, pair_kind, pair_image)],
      tiles, mapped, kern_t, adjoint, radial_near, packed, slope)

    mix_rows, mix_cols = channels // n_dom, channels // n_rep
    results = pl.pallas_call(
        functools.partial(return_kernel, n_dom, n_rep),
        out_shape=(shape((atoms, channels), BF16), shape((3, atoms), F32), shape((6, atoms), F32),
                   shape((mix_rows, mix_cols), F32)),
        in_specs=[VMEM] * 4,
        out_specs=(VMEM,) * 4,
        scratch_shapes=[
            pltpu.VMEM((3, 2, TILE, channels // 2), BF16), pltpu.VMEM((3, 16, TILE), F32),
            pltpu.VMEM((3, 2, TILE, channels // 2), BF16), pltpu.VMEM((3, 16, TILE), F32),
            pltpu.VMEM((3, 2, TILE, channels // 2), BF16), pltpu.VMEM((3, 2, 16, TILE), F32),
            pltpu.VMEM((n_dom, mix_rows, mix_cols), F32), pltpu.VMEM((n_rep, atoms, channels // 2), BF16),
            pltpu.VMEM((16, atoms), F32), pltpu.VMEM((16, atoms), F32),
            *[dma((3,)) for _ in range(4)], *[dma((3, 2)) for _ in range(4)],
            dma((n_dom,)), dma((n_dom,)), dma((n_rep,)), dma((n_rep,)), dma, dma,
        ],
        compiler_params=params(2),
        name="return_gradients",
    )(gfeat, side, mix, send_rows)
    return pl.pallas_call(
        copy_out,
        out_shape=tuple(shape(a.shape, a.dtype) for a in results),
        in_specs=[VMEM] * 4,
        out_specs=(HBM,) * 4,
        scratch_shapes=[dma((4,))],
        compiler_params=pltpu.CompilerParams(vmem_limit_bytes=4 << 20),
        name="copy_out",
    )(*results)


def solution(mesh):
    in_specs = (
        P("dom", None),
        P(None, "dom"),
        P(),
        P(),
        P(),
        P(),
        P(None, "dom"),
        P(("dom", "rep")),
        P(("dom", "rep")),
        P(("dom", "rep")),
        P(None, ("dom", "rep")),
    )
    out_specs = (P("dom", None), P(None, "dom"), P(None, "dom"), P("dom", "rep"))
    body = functools.partial(on_device, mesh.shape["dom"], mesh.shape["rep"])
    return jax.shard_map(body, mesh=mesh, in_specs=in_specs, out_specs=out_specs, check_vma=False)
```

```python
import functools

import jax
import jax.numpy as jnp
from jax import lax
from jax.experimental import pallas as pl
from jax.experimental.pallas import tpu as pltpu
from jax.sharding import PartitionSpec as P

TILE = 128
OFFSETS = (1, -1, 2, -2)
CELL = 2.0
GROUP = 4
BACK_GROUP = 8
WIDE = 8
F32 = jnp.float32
BF16 = jnp.bfloat16
MESH = pl.DeviceIdType.MESH
VMEM = pl.BlockSpec(memory_space=pltpu.VMEM)
HBM = pl.BlockSpec(memory_space=pltpu.HBM)


def nt(a, b):
    return lax.dot_general(a, b, (((1,), (1,)), ((), ())), preferred_element_type=F32)


def tn(a, b):
    return lax.dot_general(a, b, (((0,), (0,)), ((), ())), preferred_element_type=F32)


def mm(a, b):
    return jnp.dot(a, b, preferred_element_type=F32)


def split3(x):
    hi = x.astype(BF16)
    rest = x - hi.astype(F32)
    mid = rest.astype(BF16)
    low = (rest - mid.astype(F32)).astype(BF16)
    return hi, mid, low


def front_kernel(n_dom, n_rep, feat_h, pos_h, rows_h, radial_h, mixing_h, readout_h, decay_h, home_h, other_h,
                 kind_h, image_h, mapped, tiles, kern_t, packed, slope, adjoint, radial,
                 feat, pos, rows, mixing, readout, decay, home, other, kind, image,
                 sendf, sendp, recvf, recvp, col, kern_f, acc, msg, recv, pk, sl,
                 load, sf, sp, rf, rp, s4, r4, s5, r5, s1, r1, s2, r2, s3, r3):
    d = lax.axis_index("dom")
    r = lax.axis_index("rep")
    loads = [pltpu.make_async_copy(src, dst, load.at[i]) for i, (src, dst) in enumerate((
        (rows_h, rows), (feat_h, feat), (pos_h, pos), (radial_h, radial), (decay_h, decay), (home_h, home),
        (other_h, other), (kind_h, kind), (image_h, image), (mixing_h, mixing), (readout_h, readout)))]
    for copy in loads:
        copy.start()
    barrier = pltpu.get_barrier_semaphore()
    c = lax.rem(r, 2)
    partner = {"dom": d, "rep": r + 1 - 2 * c}
    steps = (c + 1, -(c + 1))
    for o in steps:
        pl.semaphore_signal(barrier, inc=1, device_id={"dom": lax.rem(d + o + n_dom, n_dom), "rep": r},
                            device_id_type=MESH)
    peers = [lax.rem(r + i, n_rep) for i in range(1, n_rep)]
    for q in peers:
        pl.semaphore_signal(barrier, inc=1, device_id={"dom": d, "rep": q}, device_id_type=MESH)
    atoms = feat.shape[0]
    own = atoms // TILE
    iota = lax.broadcasted_iota(jnp.int32, (atoms, TILE), 0)
    for copy in loads[:3]:
        copy.wait()
    copies = []
    hots = []
    for q in range(2):
        hot = (iota == rows[pl.ds(2 * c + q, 1), :]).astype(F32)
        hots.append(hot.astype(BF16))
        sendp[q] = jnp.dot(pos[...], hot, precision=lax.Precision.HIGHEST, preferred_element_type=F32)
    pl.semaphore_wait(barrier, 2 + n_rep - 1)
    targets = [{"dom": lax.rem(d + o + n_dom, n_dom), "rep": r} for o in steps]
    for src, dst, ss, rs in ((sendp, recvp, sp, rp), (sendf, recvf, sf, rf)):
        for q in range(2):
            t = 2 * c + q
            if src is sendf:
                sendf[q] = tn(hots[q], feat[...]).astype(BF16)
            copies.append(pltpu.make_async_remote_copy(src.at[q], dst.at[t], ss.at[q], rs.at[t],
                                                       device_id=targets[q], device_id_type=MESH))
            copies[-1].start()

    def columns(j):
        for c in range(3):
            col[j, c] = jnp.transpose(jnp.broadcast_to(tiles[j][c:c + 1, :], (TILE, TILE)))

    for copy in loads[3:]:
        copy.wait()
    for j in range(own):
        tiles[j] = pos[:, j * TILE:(j + 1) * TILE]
        columns(j)

    def local(k, _):
        res = mm(feat[...], radial[k]).astype(BF16)
        for j in range(own):
            mapped[j, k] = res[j * TILE:(j + 1) * TILE]
        return 0

    lax.fori_loop(0, radial.shape[0], local, 0)
    def distant(base, k):
        both = recvf[pl.ds(base, 2)].reshape(2 * TILE, -1)
        res = mm(both, radial[k]).astype(BF16)
        mapped[own + base, k] = res[:TILE]
        mapped[own + base + 1, k] = res[TILE:]

    def spread(base):
        lax.fori_loop(0, radial.shape[0], lambda k, _: (distant(base, k), 0)[1], 0)

    relays = []

    def relay(buf, first, ss, rs):
        for q in range(2):
            t = 2 * c + q
            copies[first + q].wait_recv()
            relays.append(pltpu.make_async_remote_copy(buf.at[t], buf.at[t], ss.at[q], rs.at[t],
                                                       device_id=partner, device_id_type=MESH))
            relays[-1].start()

    def relayed(buf, ss, rs):
        for q in range(2):
            t = 2 * (1 - c) + q
            pltpu.make_async_remote_copy(buf.at[t], buf.at[t], ss.at[q], rs.at[t],
                                         device_id=partner, device_id_type=MESH).wait_recv()

    pairs = home.shape[0]
    steps_all = pairs // GROUP

    def kernels(g, _):
        for u in range(GROUP):
            p = g * GROUP + u
            h, o, k = home[p], other[p], kind[p]
            row = tiles[o]
            d2 = None
            for x in range(3):
                sep = (row[x:x + 1, :] + image[x, p].astype(F32) * CELL) - col[h, x]
                d2 = sep * sep if d2 is None else d2 + sep * sep
            kern = jnp.exp(d2 * (-decay[k]))
            for i in range(own):
                kern_f[p, i * TILE:(i + 1) * TILE, :] = (kern * (h == i).astype(F32)).astype(BF16)
        return 0

    relay(recvp, 0, s5, r5)
    relayed(recvp, s5, r5)
    for t in range(4):
        tiles[own + t] = recvp[t]
        columns(own + t)
    lax.fori_loop(0, steps_all // 2, kernels, 0)
    relay(recvf, 2, s4, r4)
    lax.fori_loop(steps_all // 2, steps_all, kernels, 0)
    spread(2 * c)
    relayed(recvf, s4, r4)
    spread(2 * (1 - c))

    acc[...] = jnp.zeros_like(acc)

    def forward(g, _):
        left = [kern_f[g * WIDE + u] for u in range(WIDE)]
        right = [mapped[other[g * WIDE + u], kind[g * WIDE + u]] for u in range(WIDE)]
        acc[...] += mm(jnp.concatenate(left, axis=1), jnp.concatenate(right, axis=0))
        return 0

    lax.fori_loop(0, pairs // WIDE, forward, 0)
    share = atoms // n_rep
    for q in range(n_rep):
        msg[q] = acc[q * share:(q + 1) * share, :].astype(BF16)

    def push(src, dst, ss, rs, q):
        copy = pltpu.make_async_remote_copy(src, dst, ss, rs, device_id={"dom": d, "rep": q},
                                            device_id_type=MESH)
        copy.start()
        return copy

    def take(dst, ss, rs, q):
        pltpu.make_async_remote_copy(dst, dst, ss, rs, device_id={"dom": d, "rep": q},
                                     device_id_type=MESH).wait_recv()

    def transposed(g, _):
        for u in range(GROUP):
            p = g * GROUP + u
            h, o, k = home[p], other[p], kind[p]
            row = tiles[h]
            d2 = None
            for c in range(3):
                sep = col[o, c] - (row[c:c + 1, :] - image[c, p].astype(F32) * CELL)
                d2 = sep * sep if d2 is None else d2 + sep * sep
            kern_t[p] = jnp.exp(d2 * (-decay[k]))
        return 0

    sent = [push(msg.at[q], recv.at[r], s1.at[i], r1.at[r], q) for i, q in enumerate(peers)]
    half = pairs // GROUP // 2
    lax.fori_loop(0, half, transposed, 0)
    total = msg[r].astype(F32)
    for i, q in enumerate(peers):
        take(recv.at[q], s1.at[i], r1.at[q], q)
        total = total + recv[q].astype(F32)
    low = total.astype(BF16)
    pk[r] = low
    mixed = mm(low, mixing[...])
    sig = jax.nn.sigmoid(mixed)
    sl[r] = (readout[...] * sig * (1.0 + mixed * (1.0 - sig))).astype(BF16)
    sent += [push(sl.at[r], sl.at[r], s3.at[i], r3.at[r], q) for i, q in enumerate(peers)]
    sent += [push(pk.at[r], pk.at[r], s2.at[i], r2.at[r], q) for i, q in enumerate(peers)]
    lax.fori_loop(half, pairs // GROUP, transposed, 0)
    for i, q in enumerate(peers):
        take(sl.at[q], s3.at[i], r3.at[q], q)
    full = sl[...].reshape(-1, mixing.shape[0])
    slope[...] = full
    adj = nt(full, mixing[...]).astype(BF16)
    for j in range(own):
        adjoint[j] = adj[j * TILE:(j + 1) * TILE]
    for i, q in enumerate(peers):
        take(pk.at[q], s2.at[i], r2.at[q], q)
    packed[...] = pk[...].reshape(-1, mixing.shape[0])
    for copy in copies + relays + sent:
        copy.wait_send()


def backward_kernel(n_rep, decay_h, home_h, other_h, kind_h, image_h, tiles, mapped, kern_t, adjoint, radial,
                    packed, slope, gfeat, side, mix, decay, home, other, kind, image, moments, first, second,
                    acc, load):
    loads = [pltpu.make_async_copy(src, dst, load.at[i]) for i, (src, dst) in enumerate((
        (decay_h, decay), (home_h, home), (other_h, other), (kind_h, kind), (image_h, image)))]
    for copy in loads:
        copy.start()
    n_ext = tiles.shape[0]
    for j in range(n_ext):
        pos = tiles[j]
        x, y, z = pos[0:1, :], pos[1:2, :], pos[2:3, :]
        zero = jnp.zeros((2, TILE), F32)
        one_rows = jnp.concatenate([x, y, z, x, x, y, zero], axis=0)
        two_rows = jnp.concatenate([x, y, z, y, z, z, zero], axis=0)
        first[j] = one_rows
        second[j] = two_rows
        stack = jnp.concatenate([one_rows * two_rows, one_rows, two_rows], axis=0)
        parts = [v.astype(F32) for v in split3(stack)]
        table = jnp.concatenate(
            [parts[0], jnp.ones((8, TILE), F32), parts[1], parts[2]], axis=0).astype(BF16)
        moments[j] = jnp.concatenate([table, table], axis=1)
    acc[...] = jnp.zeros_like(acc)
    side[...] = jnp.zeros_like(side)
    sub = lax.broadcasted_iota(jnp.int32, (8, TILE), 0)

    def rows_of(a, b):
        return ((sub == a[0]) | (sub == a[1]) | (sub == a[2])), ((sub == b[0]) | (sub == b[1]))

    is_x1, is_y1 = rows_of((0, 3, 4), (1, 5))
    is_x2, is_y2 = (sub == 0), ((sub == 1) | (sub == 3))

    def fold(res):
        quad = res[0:8] + res[32:40] + res[56:64]
        lin1 = res[8:16] + res[40:48] + res[64:72]
        lin2 = res[16:24] + res[48:56] + res[72:80]
        return quad, lin1, lin2, res[24:32]

    def combine(res, a, b):
        quad, lin1, lin2, one = fold(res)
        force = lin1 - a * one
        virial = -0.5 * (quad - a * lin2 - b * lin1 + a * b * one)
        return jnp.concatenate([force, virial], axis=0)

    for copy in loads:
        copy.wait()

    def body(g, _):
        found = []
        names = []
        weights = []
        for u in range(BACK_GROUP):
            p = g * BACK_GROUP + u
            h, o, k = home[p], other[p], kind[p]
            names.append((p, h, o, k))
            kern = kern_t[p]
            weight = (-2.0 * decay[k]) * kern * nt(mapped[o, k], adjoint[h])
            hi = weight.astype(BF16)
            lo = (weight - hi.astype(F32)).astype(BF16)
            weights.append((hi, lo))
        for (p, h, o, k), (hi, lo) in zip(names, weights):
            back = mm(kern_t[p].astype(BF16), adjoint[h]).astype(BF16)
            part = nt(back, radial[k])
            shift = [image[c, p].astype(F32) * CELL for c in range(3)]
            near_res = mm(moments[o], jnp.concatenate([hi, lo], axis=0))
            far_res = nt(moments[h], jnp.concatenate([hi, lo], axis=1))
            s1 = jnp.where(is_x1, shift[0], jnp.where(is_y1, shift[1], shift[2]))
            s2 = jnp.where(is_x2, shift[0], jnp.where(is_y2, shift[1], shift[2]))
            near_side = combine(near_res, first[h] - s1, second[h] - s2)
            far_side = combine(far_res, first[o] + s1, second[o] + s2)
            found.append((h, o, part, near_side, far_side))
        for h, o, part, near_side, far_side in found:
            acc[o] += part
            side[h] += near_side
            side[o] += far_side
        return 0

    lax.fori_loop(0, home.shape[0] // BACK_GROUP, body, 0)
    for j in range(n_ext):
        for half in range(2):
            gfeat[j, half] = acc[j, :, half * TILE:(half + 1) * TILE].astype(BF16)
    r = lax.axis_index("rep")
    channels = slope.shape[1]
    share = channels // n_rep
    pick = (lax.broadcasted_iota(jnp.int32, (channels, share), 0)
            == lax.broadcasted_iota(jnp.int32, (channels, share), 1) + r * share).astype(BF16)
    cols = mm(slope[...], pick).astype(BF16)
    res = tn(packed[...], cols)
    mix[...] = res.reshape(mix.shape)


def return_kernel(n_dom, n_rep, gfeat, side, mix, rows, out_feat, out_force, out_virial, out_mix,
                  gp, gs, sb, ss, rf, rs, rm, part, pside, qside,
                  sem_gf, sem_hf, sem_gs, sem_hs, sem_sf, sem_rf, sem_ss, sem_rs, sem_sm, sem_rm, sem_sp, sem_rp, sem_sq, sem_rq):
    d = lax.axis_index("dom")
    r = lax.axis_index("rep")
    y = lax.div(r, 2)
    c = lax.rem(r, 2)

    def dom_at(o):
        return lax.rem(d + o + n_dom, n_dom)

    barrier = pltpu.get_barrier_semaphore()

    def hello(dom, rep):
        pl.semaphore_signal(barrier, inc=1, device_id={"dom": dom, "rep": rep}, device_id_type=MESH)

    mine = [(c + 1), -(c + 1)]
    peers = [lax.rem(r + i, n_rep) for i in range(1, n_rep)]
    for o in mine:
        for half in range(n_rep // 2):
            hello(dom_at(o), 2 * half + c)
    for q in peers:
        hello(d, q)

    def greet(i, _):
        hello(lax.rem(d + i, n_dom), r)
        return 0

    lax.fori_loop(1, n_dom, greet, 0)
    pl.semaphore_wait(barrier, n_rep + n_rep - 1 + n_dom - 1)

    partner = {"dom": d, "rep": r + 1 - 2 * c}
    mate = 1 - c
    sends = []
    swaps = []
    for slot, j in ((1, 2 + 2 * mate), (2, 3 + 2 * mate), (0, mate)):
        cf = pltpu.make_async_remote_copy(gfeat.at[j], gp.at[slot], sem_gf.at[slot], sem_hf.at[slot],
                                          device_id=partner, device_id_type=MESH)
        cs = pltpu.make_async_remote_copy(side.at[j], gs.at[slot], sem_gs.at[slot], sem_hs.at[slot],
                                          device_id=partner, device_id_type=MESH)
        cf.start()
        cs.start()
        swaps.append((cf, cs))
        sends += [cf, cs]
    for (cf, cs), (slot, j) in zip(swaps, ((1, 2 + 2 * c), (2, 3 + 2 * c), (0, c))):
        cf.wait_recv()
        cs.wait_recv()
        sb[slot] = (gfeat[j].astype(F32) + gp[slot].astype(F32)).astype(BF16)
        ss[slot] = side[j] + gs[slot]
        for half in ((0, 1) if slot else (1 - y,)):
            dest = {"dom": dom_at(-mine[slot - 1]) if slot else d, "rep": 2 * half + c}
            nf = pltpu.make_async_remote_copy(sb.at[slot, half], rf.at[slot, y], sem_sf.at[slot, half],
                                              sem_rf.at[slot, y], device_id=dest, device_id_type=MESH)
            ns = pltpu.make_async_remote_copy(ss.at[slot], rs.at[slot, y], sem_ss.at[slot, half],
                                              sem_rs.at[slot, y], device_id=dest, device_id_type=MESH)
            nf.start()
            ns.start()
            sends += [nf, ns]

    def mix_copy(i):
        to = lax.rem(d + i, n_dom)
        return pltpu.make_async_remote_copy(mix.at[to], rm.at[d], sem_sm.at[i], sem_rm.at[d],
                                            device_id={"dom": to, "rep": r}, device_id_type=MESH)

    def mix_start(i, _):
        mix_copy(i).start()
        return 0

    lax.fori_loop(1, n_dom, mix_start, 0)

    def take(dst, ss, rsem):
        pltpu.make_async_remote_copy(dst, dst, ss, rsem, device_id={"dom": d, "rep": peers[0]},
                                     device_id_type=MESH).wait_recv()

    take(rf.at[0, 1 - y], sem_sf.at[0, 0], sem_rf.at[0, 1 - y])
    take(rs.at[0, 1 - y], sem_ss.at[0, 0], sem_rs.at[0, 1 - y])
    feat_self = sb[0, y].astype(F32) + rf[0, 1 - y].astype(F32)
    side_self = ss[0] + rs[0, 1 - y]
    is_low = c == 0
    zero = jnp.zeros_like(feat_self)
    total = jnp.concatenate([jnp.where(is_low, feat_self, zero), jnp.where(is_low, zero, feat_self)], axis=0)
    zside = jnp.zeros_like(side_self)
    total_side = jnp.concatenate([jnp.where(is_low, side_self, zside), jnp.where(is_low, zside, side_self)],
                                 axis=1)
    atoms = out_feat.shape[0]
    iota = lax.broadcasted_iota(jnp.int32, (atoms, TILE), 0)
    for q in range(2):
        hot = (iota == rows[pl.ds(2 * c + q, 1), :]).astype(F32).astype(BF16)
        slot = 1 + q
        got = None
        for s in range(n_rep // 2):
            take(rf.at[slot, s], sem_sf.at[0, 0], sem_rf.at[slot, s])
            take(rs.at[slot, s], sem_ss.at[0, 0], sem_rs.at[slot, s])
            total = total + mm(hot, rf[slot, s])
            got = rs[slot, s] if got is None else got + rs[slot, s]
        for v in split3(got):
            total_side = total_side + nt(v, hot)
    part[r] = total.astype(BF16)
    pside[...] = total_side
    phase = []
    for i, q in enumerate(peers):
        cp = pltpu.make_async_remote_copy(part.at[r], part.at[r], sem_sp.at[i], sem_rp.at[r],
                                          device_id={"dom": d, "rep": q}, device_id_type=MESH)
        cp.start()
        phase.append(cp)
    cq = pltpu.make_async_remote_copy(pside, qside, sem_sq, sem_rq,
                                      device_id={"dom": d, "rep": r + 1 - 2 * c}, device_id_type=MESH)
    cq.start()

    def mix_add(i, value):
        frm = lax.rem(d + i, n_dom)
        take(rm.at[frm], sem_sm.at[0], sem_rm.at[frm])
        return value + rm[frm]

    out_mix[...] = lax.fori_loop(1, n_dom, mix_add, mix[d])
    cq.wait_recv()
    final = total_side + qside[...]
    out_force[...] = final[0:3]
    out_virial[...] = final[8:14]
    for q in peers:
        take(part.at[q], sem_sp.at[0], sem_rp.at[q])
    for half in range(2):
        out_feat[:, half * TILE:(half + 1) * TILE] = (
            part[2 * half].astype(F32) + part[2 * half + 1].astype(F32)).astype(BF16)
    for copy in sends:
        copy.wait_send()

    def mix_done(i, _):
        mix_copy(i).wait_send()
        return 0

    lax.fori_loop(1, n_dom, mix_done, 0)
    for cp in phase:
        cp.wait_send()
    cq.wait_send()


def copy_out(a, b, c, d, a_h, b_h, c_h, d_h, sem):
    copies = [pltpu.make_async_copy(src, dst, sem.at[i])
              for i, (src, dst) in enumerate(((a, a_h), (b, b_h), (c, c_h), (d, d_h)))]
    for copy in copies:
        copy.start()
    for copy in copies:
        copy.wait()


def on_device(n_dom, n_rep, features, positions, radial, mixing, readout, decay, send_rows, pair_home,
              pair_other, pair_kind, pair_image):
    atoms, channels = features.shape
    own = atoms // TILE
    n_ext = own + len(OFFSETS)
    kinds = radial.shape[0]
    dma = pltpu.SemaphoreType.DMA
    share = atoms // n_rep

    def params(cid=None):
        if cid is None:
            return pltpu.CompilerParams(vmem_limit_bytes=40 << 20)
        return pltpu.CompilerParams(collective_id=cid, has_side_effects=True, vmem_limit_bytes=40 << 20)

    def shape(dims, dtype):
        return jax.ShapeDtypeStruct(dims, dtype)

    def pair_tables():
        return [pltpu.SMEM(decay.shape, F32)] + [
            pltpu.SMEM(a.shape, jnp.int32) for a in (pair_home, pair_other, pair_kind, pair_image)]

    readout_row = readout.reshape(1, channels)
    mapped, tiles, kern_t, packed, slope, adjoint, radial_near = pl.pallas_call(
        functools.partial(front_kernel, n_dom, n_rep),
        out_shape=(shape((n_ext, kinds, TILE, channels), BF16), shape((n_ext, 3, TILE), F32),
                   shape((pair_home.shape[0], TILE, TILE), F32), shape((atoms, channels), BF16),
                   shape((atoms, channels), BF16), shape((own, TILE, channels), BF16),
                   shape(radial.shape, BF16)),
        in_specs=[HBM] * 11,
        out_specs=(VMEM,) * 7,
        scratch_shapes=[
            pltpu.VMEM(features.shape, BF16), pltpu.VMEM(positions.shape, F32),
            pltpu.VMEM(send_rows.shape, jnp.int32),
            pltpu.VMEM(mixing.shape, BF16), pltpu.VMEM(readout_row.shape, F32), *pair_tables(),
            pltpu.VMEM((2, TILE, channels), BF16), pltpu.VMEM((2, 3, TILE), F32),
            pltpu.VMEM((4, TILE, channels), BF16), pltpu.VMEM((4, 3, TILE), F32),
            pltpu.VMEM((n_ext, 3, TILE, TILE), F32),
            pltpu.VMEM((pair_home.shape[0], atoms, TILE), BF16), pltpu.VMEM((atoms, channels), F32),
            *[pltpu.VMEM((n_rep, share, channels), BF16)] * 4,
            dma((11,)), *[dma((4,)) for _ in range(8)], *[dma((n_rep,)) for _ in range(6)],
        ],
        compiler_params=params(0),
        name="front",
    )(*[pltpu.with_memory_space_constraint(a, pltpu.HBM) for a in (
        features, positions, send_rows, radial, mixing, readout_row, decay, pair_home, pair_other, pair_kind,
        pair_image)])

    gfeat, side, mix = pl.pallas_call(
        functools.partial(backward_kernel, n_rep),
        out_shape=(shape((n_ext, 2, TILE, channels // 2), BF16), shape((n_ext, 16, TILE), F32),
                   shape((n_dom, channels // n_dom, channels // n_rep), F32)),
        in_specs=[HBM] * 5 + [VMEM] * 7,
        out_specs=(VMEM,) * 3,
        scratch_shapes=[
            *pair_tables(), pltpu.VMEM((n_ext, 80, 2 * TILE), BF16),
            pltpu.VMEM((n_ext, 8, TILE), F32), pltpu.VMEM((n_ext, 8, TILE), F32),
            pltpu.VMEM((n_ext, TILE, channels), F32), dma((5,)),
        ],
        compiler_params=params(),
        name="backward_pairs",
    )(*[pltpu.with_memory_space_constraint(a, pltpu.HBM) for a in (
        decay, pair_home, pair_other, pair_kind, pair_image)],
      tiles, mapped, kern_t, adjoint, radial_near, packed, slope)

    mix_rows, mix_cols = channels // n_dom, channels // n_rep
    results = pl.pallas_call(
        functools.partial(return_kernel, n_dom, n_rep),
        out_shape=(shape((atoms, channels), BF16), shape((3, atoms), F32), shape((6, atoms), F32),
                   shape((mix_rows, mix_cols), F32)),
        in_specs=[VMEM] * 4,
        out_specs=(VMEM,) * 4,
        scratch_shapes=[
            pltpu.VMEM((3, 2, TILE, channels // 2), BF16), pltpu.VMEM((3, 16, TILE), F32),
            pltpu.VMEM((3, 2, TILE, channels // 2), BF16), pltpu.VMEM((3, 16, TILE), F32),
            pltpu.VMEM((3, 2, TILE, channels // 2), BF16), pltpu.VMEM((3, 2, 16, TILE), F32),
            pltpu.VMEM((n_dom, mix_rows, mix_cols), F32), pltpu.VMEM((n_rep, atoms, channels // 2), BF16),
            pltpu.VMEM((16, atoms), F32), pltpu.VMEM((16, atoms), F32),
            *[dma((3,)) for _ in range(4)], *[dma((3, 2)) for _ in range(4)],
            dma((n_dom,)), dma((n_dom,)), dma((n_rep,)), dma((n_rep,)), dma, dma,
        ],
        compiler_params=params(2),
        name="return_gradients",
    )(gfeat, side, mix, send_rows)
    return pl.pallas_call(
        copy_out,
        out_shape=tuple(shape(a.shape, a.dtype) for a in results),
        in_specs=[VMEM] * 4,
        out_specs=(HBM,) * 4,
        scratch_shapes=[dma((4,))],
        compiler_params=pltpu.CompilerParams(vmem_limit_bytes=4 << 20),
        name="copy_out",
    )(*results)


def solution(mesh):
    in_specs = (
        P("dom", None),
        P(None, "dom"),
        P(),
        P(),
        P(),
        P(),
        P(None, "dom"),
        P(("dom", "rep")),
        P(("dom", "rep")),
        P(("dom", "rep")),
        P(None, ("dom", "rep")),
    )
    out_specs = (P("dom", None), P(None, "dom"), P(None, "dom"), P("dom", "rep"))
    body = functools.partial(on_device, mesh.shape["dom"], mesh.shape["rep"])
    return jax.shard_map(body, mesh=mesh, in_specs=in_specs, out_specs=out_specs, check_vma=False)
```

```python
import functools

import jax
import jax.numpy as jnp
from jax import lax
from jax.experimental import pallas as pl
from jax.experimental.pallas import tpu as pltpu
from jax.sharding import PartitionSpec as P

TILE = 128
OFFSETS = (1, -1, 2, -2)
CELL = 2.0
GROUP = 4
BACK_GROUP = 12
WIDE = 8
F32 = jnp.float32
BF16 = jnp.bfloat16
MESH = pl.DeviceIdType.MESH
VMEM = pl.BlockSpec(memory_space=pltpu.VMEM)
HBM = pl.BlockSpec(memory_space=pltpu.HBM)


def nt(a, b):
    return lax.dot_general(a, b, (((1,), (1,)), ((), ())), preferred_element_type=F32)


def tn(a, b):
    return lax.dot_general(a, b, (((0,), (0,)), ((), ())), preferred_element_type=F32)


def mm(a, b):
    return jnp.dot(a, b, preferred_element_type=F32)


def split3(x):
    hi = x.astype(BF16)
    rest = x - hi.astype(F32)
    mid = rest.astype(BF16)
    low = (rest - mid.astype(F32)).astype(BF16)
    return hi, mid, low


def front_kernel(n_dom, n_rep, feat_h, pos_h, rows_h, radial_h, mixing_h, readout_h, decay_h, home_h, other_h,
                 kind_h, image_h, mapped, tiles, kern_t, packed, slope, adjoint, radial,
                 feat, pos, rows, mixing, readout, decay, home, other, kind, image,
                 sendf, sendp, recvf, recvp, col, kern_f, acc, msg, recv, pk, sl,
                 load, sf, sp, rf, rp, s4, r4, s5, r5, s1, r1, s2, r2, s3, r3):
    d = lax.axis_index("dom")
    r = lax.axis_index("rep")
    loads = [pltpu.make_async_copy(src, dst, load.at[i]) for i, (src, dst) in enumerate((
        (rows_h, rows), (feat_h, feat), (pos_h, pos), (radial_h, radial), (decay_h, decay), (home_h, home),
        (other_h, other), (kind_h, kind), (image_h, image), (mixing_h, mixing), (readout_h, readout)))]
    for copy in loads:
        copy.start()
    barrier = pltpu.get_barrier_semaphore()
    c = lax.rem(r, 2)
    partner = {"dom": d, "rep": r + 1 - 2 * c}
    steps = (c + 1, -(c + 1))
    for o in steps:
        pl.semaphore_signal(barrier, inc=1, device_id={"dom": lax.rem(d + o + n_dom, n_dom), "rep": r},
                            device_id_type=MESH)
    peers = [lax.rem(r + i, n_rep) for i in range(1, n_rep)]
    for q in peers:
        pl.semaphore_signal(barrier, inc=1, device_id={"dom": d, "rep": q}, device_id_type=MESH)
    atoms = feat.shape[0]
    own = atoms // TILE
    iota = lax.broadcasted_iota(jnp.int32, (atoms, TILE), 0)
    for copy in loads[:3]:
        copy.wait()
    copies = []
    hots = []
    for q in range(2):
        hot = (iota == rows[pl.ds(2 * c + q, 1), :]).astype(F32)
        hots.append(hot.astype(BF16))
        sendp[q] = jnp.dot(pos[...], hot, precision=lax.Precision.HIGHEST, preferred_element_type=F32)
    pl.semaphore_wait(barrier, 2 + n_rep - 1)
    targets = [{"dom": lax.rem(d + o + n_dom, n_dom), "rep": r} for o in steps]
    for src, dst, ss, rs in ((sendp, recvp, sp, rp), (sendf, recvf, sf, rf)):
        for q in range(2):
            t = 2 * c + q
            if src is sendf:
                sendf[q] = tn(hots[q], feat[...]).astype(BF16)
            copies.append(pltpu.make_async_remote_copy(src.at[q], dst.at[t], ss.at[q], rs.at[t],
                                                       device_id=targets[q], device_id_type=MESH))
            copies[-1].start()

    def columns(j):
        for c in range(3):
            col[j, c] = jnp.transpose(jnp.broadcast_to(tiles[j][c:c + 1, :], (TILE, TILE)))

    for copy in loads[3:]:
        copy.wait()
    for j in range(own):
        tiles[j] = pos[:, j * TILE:(j + 1) * TILE]
        columns(j)

    def local(k, _):
        res = mm(feat[...], radial[k]).astype(BF16)
        for j in range(own):
            mapped[j, k] = res[j * TILE:(j + 1) * TILE]
        return 0

    lax.fori_loop(0, radial.shape[0], local, 0)
    def distant(base, k):
        both = recvf[pl.ds(base, 2)].reshape(2 * TILE, -1)
        res = mm(both, radial[k]).astype(BF16)
        mapped[own + base, k] = res[:TILE]
        mapped[own + base + 1, k] = res[TILE:]

    def spread(base):
        lax.fori_loop(0, radial.shape[0], lambda k, _: (distant(base, k), 0)[1], 0)

    relays = []

    def relay(buf, first, ss, rs):
        for q in range(2):
            t = 2 * c + q
            copies[first + q].wait_recv()
            relays.append(pltpu.make_async_remote_copy(buf.at[t], buf.at[t], ss.at[q], rs.at[t],
                                                       device_id=partner, device_id_type=MESH))
            relays[-1].start()

    def relayed(buf, ss, rs):
        for q in range(2):
            t = 2 * (1 - c) + q
            pltpu.make_async_remote_copy(buf.at[t], buf.at[t], ss.at[q], rs.at[t],
                                         device_id=partner, device_id_type=MESH).wait_recv()

    pairs = home.shape[0]
    steps_all = pairs // GROUP

    def kernels(g, _):
        for u in range(GROUP):
            p = g * GROUP + u
            h, o, k = home[p], other[p], kind[p]
            row = tiles[o]
            d2 = None
            for x in range(3):
                sep = (row[x:x + 1, :] + image[x, p].astype(F32) * CELL) - col[h, x]
                d2 = sep * sep if d2 is None else d2 + sep * sep
            kern = jnp.exp(d2 * (-decay[k]))
            for i in range(own):
                kern_f[p, i * TILE:(i + 1) * TILE, :] = (kern * (h == i).astype(F32)).astype(BF16)
        return 0

    relay(recvp, 0, s5, r5)
    relayed(recvp, s5, r5)
    for t in range(4):
        tiles[own + t] = recvp[t]
        columns(own + t)
    lax.fori_loop(0, steps_all // 2, kernels, 0)
    relay(recvf, 2, s4, r4)
    lax.fori_loop(steps_all // 2, steps_all, kernels, 0)
    spread(2 * c)
    relayed(recvf, s4, r4)
    spread(2 * (1 - c))

    acc[...] = jnp.zeros_like(acc)

    def forward(g, _):
        left = [kern_f[g * WIDE + u] for u in range(WIDE)]
        right = [mapped[other[g * WIDE + u], kind[g * WIDE + u]] for u in range(WIDE)]
        acc[...] += mm(jnp.concatenate(left, axis=1), jnp.concatenate(right, axis=0))
        return 0

    lax.fori_loop(0, pairs // WIDE, forward, 0)
    share = atoms // n_rep
    for q in range(n_rep):
        msg[q] = acc[q * share:(q + 1) * share, :].astype(BF16)

    def push(src, dst, ss, rs, q):
        copy = pltpu.make_async_remote_copy(src, dst, ss, rs, device_id={"dom": d, "rep": q},
                                            device_id_type=MESH)
        copy.start()
        return copy

    def take(dst, ss, rs, q):
        pltpu.make_async_remote_copy(dst, dst, ss, rs, device_id={"dom": d, "rep": q},
                                     device_id_type=MESH).wait_recv()

    def transposed(g, _):
        for u in range(GROUP):
            p = g * GROUP + u
            h, o, k = home[p], other[p], kind[p]
            row = tiles[h]
            d2 = None
            for c in range(3):
                sep = col[o, c] - (row[c:c + 1, :] - image[c, p].astype(F32) * CELL)
                d2 = sep * sep if d2 is None else d2 + sep * sep
            kern_t[p] = jnp.exp(d2 * (-decay[k]))
        return 0

    sent = [push(msg.at[q], recv.at[r], s1.at[i], r1.at[r], q) for i, q in enumerate(peers)]
    half = pairs // GROUP // 2
    lax.fori_loop(0, half, transposed, 0)
    total = msg[r].astype(F32)
    for i, q in enumerate(peers):
        take(recv.at[q], s1.at[i], r1.at[q], q)
        total = total + recv[q].astype(F32)
    low = total.astype(BF16)
    pk[r] = low
    mixed = mm(low, mixing[...])
    sig = jax.nn.sigmoid(mixed)
    sl[r] = (readout[...] * sig * (1.0 + mixed * (1.0 - sig))).astype(BF16)
    sent += [push(sl.at[r], sl.at[r], s3.at[i], r3.at[r], q) for i, q in enumerate(peers)]
    sent += [push(pk.at[r], pk.at[r], s2.at[i], r2.at[r], q) for i, q in enumerate(peers)]
    lax.fori_loop(half, pairs // GROUP, transposed, 0)
    for i, q in enumerate(peers):
        take(sl.at[q], s3.at[i], r3.at[q], q)
    full = sl[...].reshape(-1, mixing.shape[0])
    slope[...] = full
    adj = nt(full, mixing[...]).astype(BF16)
    for j in range(own):
        adjoint[j] = adj[j * TILE:(j + 1) * TILE]
    for i, q in enumerate(peers):
        take(pk.at[q], s2.at[i], r2.at[q], q)
    packed[...] = pk[...].reshape(-1, mixing.shape[0])
    for copy in copies + relays + sent:
        copy.wait_send()


def backward_kernel(n_rep, decay_h, home_h, other_h, kind_h, image_h, tiles, mapped, kern_t, adjoint, radial,
                    packed, slope, gfeat, side, mix, decay, home, other, kind, image, moments, first, second,
                    acc, load):
    loads = [pltpu.make_async_copy(src, dst, load.at[i]) for i, (src, dst) in enumerate((
        (decay_h, decay), (home_h, home), (other_h, other), (kind_h, kind), (image_h, image)))]
    for copy in loads:
        copy.start()
    n_ext = tiles.shape[0]
    for j in range(n_ext):
        pos = tiles[j]
        x, y, z = pos[0:1, :], pos[1:2, :], pos[2:3, :]
        zero = jnp.zeros((2, TILE), F32)
        one_rows = jnp.concatenate([x, y, z, x, x, y, zero], axis=0)
        two_rows = jnp.concatenate([x, y, z, y, z, z, zero], axis=0)
        first[j] = one_rows
        second[j] = two_rows
        stack = jnp.concatenate([one_rows * two_rows, one_rows, two_rows], axis=0)
        parts = [v.astype(F32) for v in split3(stack)]
        table = jnp.concatenate(
            [parts[0], jnp.ones((8, TILE), F32), parts[1], parts[2]], axis=0).astype(BF16)
        moments[j] = jnp.concatenate([table, table], axis=1)
    acc[...] = jnp.zeros_like(acc)
    side[...] = jnp.zeros_like(side)
    sub = lax.broadcasted_iota(jnp.int32, (8, TILE), 0)

    def rows_of(a, b):
        return ((sub == a[0]) | (sub == a[1]) | (sub == a[2])), ((sub == b[0]) | (sub == b[1]))

    is_x1, is_y1 = rows_of((0, 3, 4), (1, 5))
    is_x2, is_y2 = (sub == 0), ((sub == 1) | (sub == 3))

    def fold(res):
        quad = res[0:8] + res[32:40] + res[56:64]
        lin1 = res[8:16] + res[40:48] + res[64:72]
        lin2 = res[16:24] + res[48:56] + res[72:80]
        return quad, lin1, lin2, res[24:32]

    def combine(res, a, b):
        quad, lin1, lin2, one = fold(res)
        force = lin1 - a * one
        virial = -0.5 * (quad - a * lin2 - b * lin1 + a * b * one)
        return jnp.concatenate([force, virial], axis=0)

    for copy in loads:
        copy.wait()

    def body(g, _):
        found = []
        names = []
        weights = []
        for u in range(BACK_GROUP):
            p = g * BACK_GROUP + u
            h, o, k = home[p], other[p], kind[p]
            names.append((p, h, o, k))
            kern = kern_t[p]
            weight = (-2.0 * decay[k]) * kern * nt(mapped[o, k], adjoint[h])
            hi = weight.astype(BF16)
            lo = (weight - hi.astype(F32)).astype(BF16)
            weights.append((hi, lo))
        for (p, h, o, k), (hi, lo) in zip(names, weights):
            back = mm(kern_t[p].astype(BF16), adjoint[h]).astype(BF16)
            part = nt(back, radial[k])
            shift = [image[c, p].astype(F32) * CELL for c in range(3)]
            near_res = mm(moments[o], jnp.concatenate([hi, lo], axis=0))
            far_res = nt(moments[h], jnp.concatenate([hi, lo], axis=1))
            s1 = jnp.where(is_x1, shift[0], jnp.where(is_y1, shift[1], shift[2]))
            s2 = jnp.where(is_x2, shift[0], jnp.where(is_y2, shift[1], shift[2]))
            near_side = combine(near_res, first[h] - s1, second[h] - s2)
            far_side = combine(far_res, first[o] + s1, second[o] + s2)
            found.append((h, o, part, near_side, far_side))
        for h, o, part, near_side, far_side in found:
            acc[o] += part
            side[h] += near_side
            side[o] += far_side
        return 0

    lax.fori_loop(0, home.shape[0] // BACK_GROUP, body, 0)
    for j in range(n_ext):
        for half in range(2):
            gfeat[j, half] = acc[j, :, half * TILE:(half + 1) * TILE].astype(BF16)
    r = lax.axis_index("rep")
    channels = slope.shape[1]
    share = channels // n_rep
    pick = (lax.broadcasted_iota(jnp.int32, (channels, share), 0)
            == lax.broadcasted_iota(jnp.int32, (channels, share), 1) + r * share).astype(BF16)
    cols = mm(slope[...], pick).astype(BF16)
    res = tn(packed[...], cols)
    mix[...] = res.reshape(mix.shape)


def return_kernel(n_dom, n_rep, gfeat, side, mix, rows, out_feat, out_force, out_virial, out_mix,
                  gp, gs, sb, ss, rf, rs, rm, part, pside, qside,
                  sem_gf, sem_hf, sem_gs, sem_hs, sem_sf, sem_rf, sem_ss, sem_rs, sem_sm, sem_rm, sem_sp, sem_rp, sem_sq, sem_rq):
    d = lax.axis_index("dom")
    r = lax.axis_index("rep")
    y = lax.div(r, 2)
    c = lax.rem(r, 2)

    def dom_at(o):
        return lax.rem(d + o + n_dom, n_dom)

    barrier = pltpu.get_barrier_semaphore()

    def hello(dom, rep):
        pl.semaphore_signal(barrier, inc=1, device_id={"dom": dom, "rep": rep}, device_id_type=MESH)

    mine = [(c + 1), -(c + 1)]
    peers = [lax.rem(r + i, n_rep) for i in range(1, n_rep)]
    for o in mine:
        for half in range(n_rep // 2):
            hello(dom_at(o), 2 * half + c)
    for q in peers:
        hello(d, q)

    def greet(i, _):
        hello(lax.rem(d + i, n_dom), r)
        return 0

    lax.fori_loop(1, n_dom, greet, 0)
    pl.semaphore_wait(barrier, n_rep + n_rep - 1 + n_dom - 1)

    partner = {"dom": d, "rep": r + 1 - 2 * c}
    mate = 1 - c
    sends = []
    swaps = []
    for slot, j in ((1, 2 + 2 * mate), (2, 3 + 2 * mate), (0, mate)):
        cf = pltpu.make_async_remote_copy(gfeat.at[j], gp.at[slot], sem_gf.at[slot], sem_hf.at[slot],
                                          device_id=partner, device_id_type=MESH)
        cs = pltpu.make_async_remote_copy(side.at[j], gs.at[slot], sem_gs.at[slot], sem_hs.at[slot],
                                          device_id=partner, device_id_type=MESH)
        cf.start()
        cs.start()
        swaps.append((cf, cs))
        sends += [cf, cs]
    for (cf, cs), (slot, j) in zip(swaps, ((1, 2 + 2 * c), (2, 3 + 2 * c), (0, c))):
        cf.wait_recv()
        cs.wait_recv()
        sb[slot] = (gfeat[j].astype(F32) + gp[slot].astype(F32)).astype(BF16)
        ss[slot] = side[j] + gs[slot]
        for half in ((0, 1) if slot else (1 - y,)):
            dest = {"dom": dom_at(-mine[slot - 1]) if slot else d, "rep": 2 * half + c}
            nf = pltpu.make_async_remote_copy(sb.at[slot, half], rf.at[slot, y], sem_sf.at[slot, half],
                                              sem_rf.at[slot, y], device_id=dest, device_id_type=MESH)
            ns = pltpu.make_async_remote_copy(ss.at[slot], rs.at[slot, y], sem_ss.at[slot, half],
                                              sem_rs.at[slot, y], device_id=dest, device_id_type=MESH)
            nf.start()
            ns.start()
            sends += [nf, ns]

    def mix_copy(i):
        to = lax.rem(d + i, n_dom)
        return pltpu.make_async_remote_copy(mix.at[to], rm.at[d], sem_sm.at[i], sem_rm.at[d],
                                            device_id={"dom": to, "rep": r}, device_id_type=MESH)

    def mix_start(i, _):
        mix_copy(i).start()
        return 0

    lax.fori_loop(1, n_dom, mix_start, 0)

    def take(dst, ss, rsem):
        pltpu.make_async_remote_copy(dst, dst, ss, rsem, device_id={"dom": d, "rep": peers[0]},
                                     device_id_type=MESH).wait_recv()

    take(rf.at[0, 1 - y], sem_sf.at[0, 0], sem_rf.at[0, 1 - y])
    take(rs.at[0, 1 - y], sem_ss.at[0, 0], sem_rs.at[0, 1 - y])
    feat_self = sb[0, y].astype(F32) + rf[0, 1 - y].astype(F32)
    side_self = ss[0] + rs[0, 1 - y]
    is_low = c == 0
    zero = jnp.zeros_like(feat_self)
    total = jnp.concatenate([jnp.where(is_low, feat_self, zero), jnp.where(is_low, zero, feat_self)], axis=0)
    zside = jnp.zeros_like(side_self)
    total_side = jnp.concatenate([jnp.where(is_low, side_self, zside), jnp.where(is_low, zside, side_self)],
                                 axis=1)
    atoms = out_feat.shape[0]
    iota = lax.broadcasted_iota(jnp.int32, (atoms, TILE), 0)
    for q in range(2):
        hot = (iota == rows[pl.ds(2 * c + q, 1), :]).astype(F32).astype(BF16)
        slot = 1 + q
        got = None
        for s in range(n_rep // 2):
            take(rf.at[slot, s], sem_sf.at[0, 0], sem_rf.at[slot, s])
            take(rs.at[slot, s], sem_ss.at[0, 0], sem_rs.at[slot, s])
            total = total + mm(hot, rf[slot, s])
            got = rs[slot, s] if got is None else got + rs[slot, s]
        for v in split3(got):
            total_side = total_side + nt(v, hot)
    part[r] = total.astype(BF16)
    pside[...] = total_side
    phase = []
    for i, q in enumerate(peers):
        cp = pltpu.make_async_remote_copy(part.at[r], part.at[r], sem_sp.at[i], sem_rp.at[r],
                                          device_id={"dom": d, "rep": q}, device_id_type=MESH)
        cp.start()
        phase.append(cp)
    cq = pltpu.make_async_remote_copy(pside, qside, sem_sq, sem_rq,
                                      device_id={"dom": d, "rep": r + 1 - 2 * c}, device_id_type=MESH)
    cq.start()

    def mix_add(i, value):
        frm = lax.rem(d + i, n_dom)
        take(rm.at[frm], sem_sm.at[0], sem_rm.at[frm])
        return value + rm[frm]

    out_mix[...] = lax.fori_loop(1, n_dom, mix_add, mix[d])
    cq.wait_recv()
    final = total_side + qside[...]
    out_force[...] = final[0:3]
    out_virial[...] = final[8:14]
    for q in peers:
        take(part.at[q], sem_sp.at[0], sem_rp.at[q])
    for half in range(2):
        out_feat[:, half * TILE:(half + 1) * TILE] = (
            part[2 * half].astype(F32) + part[2 * half + 1].astype(F32)).astype(BF16)
    for copy in sends:
        copy.wait_send()

    def mix_done(i, _):
        mix_copy(i).wait_send()
        return 0

    lax.fori_loop(1, n_dom, mix_done, 0)
    for cp in phase:
        cp.wait_send()
    cq.wait_send()


def copy_out(a, b, c, d, a_h, b_h, c_h, d_h, sem):
    copies = [pltpu.make_async_copy(src, dst, sem.at[i])
              for i, (src, dst) in enumerate(((a, a_h), (b, b_h), (c, c_h), (d, d_h)))]
    for copy in copies:
        copy.start()
    for copy in copies:
        copy.wait()


def on_device(n_dom, n_rep, features, positions, radial, mixing, readout, decay, send_rows, pair_home,
              pair_other, pair_kind, pair_image):
    atoms, channels = features.shape
    own = atoms // TILE
    n_ext = own + len(OFFSETS)
    kinds = radial.shape[0]
    dma = pltpu.SemaphoreType.DMA
    share = atoms // n_rep

    def params(cid=None):
        if cid is None:
            return pltpu.CompilerParams(vmem_limit_bytes=40 << 20)
        return pltpu.CompilerParams(collective_id=cid, has_side_effects=True, vmem_limit_bytes=40 << 20)

    def shape(dims, dtype):
        return jax.ShapeDtypeStruct(dims, dtype)

    def pair_tables():
        return [pltpu.SMEM(decay.shape, F32)] + [
            pltpu.SMEM(a.shape, jnp.int32) for a in (pair_home, pair_other, pair_kind, pair_image)]

    readout_row = readout.reshape(1, channels)
    mapped, tiles, kern_t, packed, slope, adjoint, radial_near = pl.pallas_call(
        functools.partial(front_kernel, n_dom, n_rep),
        out_shape=(shape((n_ext, kinds, TILE, channels), BF16), shape((n_ext, 3, TILE), F32),
                   shape((pair_home.shape[0], TILE, TILE), F32), shape((atoms, channels), BF16),
                   shape((atoms, channels), BF16), shape((own, TILE, channels), BF16),
                   shape(radial.shape, BF16)),
        in_specs=[HBM] * 11,
        out_specs=(VMEM,) * 7,
        scratch_shapes=[
            pltpu.VMEM(features.shape, BF16), pltpu.VMEM(positions.shape, F32),
            pltpu.VMEM(send_rows.shape, jnp.int32),
            pltpu.VMEM(mixing.shape, BF16), pltpu.VMEM(readout_row.shape, F32), *pair_tables(),
            pltpu.VMEM((2, TILE, channels), BF16), pltpu.VMEM((2, 3, TILE), F32),
            pltpu.VMEM((4, TILE, channels), BF16), pltpu.VMEM((4, 3, TILE), F32),
            pltpu.VMEM((n_ext, 3, TILE, TILE), F32),
            pltpu.VMEM((pair_home.shape[0], atoms, TILE), BF16), pltpu.VMEM((atoms, channels), F32),
            *[pltpu.VMEM((n_rep, share, channels), BF16)] * 4,
            dma((11,)), *[dma((4,)) for _ in range(8)], *[dma((n_rep,)) for _ in range(6)],
        ],
        compiler_params=params(0),
        name="front",
    )(*[pltpu.with_memory_space_constraint(a, pltpu.HBM) for a in (
        features, positions, send_rows, radial, mixing, readout_row, decay, pair_home, pair_other, pair_kind,
        pair_image)])

    gfeat, side, mix = pl.pallas_call(
        functools.partial(backward_kernel, n_rep),
        out_shape=(shape((n_ext, 2, TILE, channels // 2), BF16), shape((n_ext, 16, TILE), F32),
                   shape((n_dom, channels // n_dom, channels // n_rep), F32)),
        in_specs=[HBM] * 5 + [VMEM] * 7,
        out_specs=(VMEM,) * 3,
        scratch_shapes=[
            *pair_tables(), pltpu.VMEM((n_ext, 80, 2 * TILE), BF16),
            pltpu.VMEM((n_ext, 8, TILE), F32), pltpu.VMEM((n_ext, 8, TILE), F32),
            pltpu.VMEM((n_ext, TILE, channels), F32), dma((5,)),
        ],
        compiler_params=params(),
        name="backward_pairs",
    )(*[pltpu.with_memory_space_constraint(a, pltpu.HBM) for a in (
        decay, pair_home, pair_other, pair_kind, pair_image)],
      tiles, mapped, kern_t, adjoint, radial_near, packed, slope)

    mix_rows, mix_cols = channels // n_dom, channels // n_rep
    results = pl.pallas_call(
        functools.partial(return_kernel, n_dom, n_rep),
        out_shape=(shape((atoms, channels), BF16), shape((3, atoms), F32), shape((6, atoms), F32),
                   shape((mix_rows, mix_cols), F32)),
        in_specs=[VMEM] * 4,
        out_specs=(VMEM,) * 4,
        scratch_shapes=[
            pltpu.VMEM((3, 2, TILE, channels // 2), BF16), pltpu.VMEM((3, 16, TILE), F32),
            pltpu.VMEM((3, 2, TILE, channels // 2), BF16), pltpu.VMEM((3, 16, TILE), F32),
            pltpu.VMEM((3, 2, TILE, channels // 2), BF16), pltpu.VMEM((3, 2, 16, TILE), F32),
            pltpu.VMEM((n_dom, mix_rows, mix_cols), F32), pltpu.VMEM((n_rep, atoms, channels // 2), BF16),
            pltpu.VMEM((16, atoms), F32), pltpu.VMEM((16, atoms), F32),
            *[dma((3,)) for _ in range(4)], *[dma((3, 2)) for _ in range(4)],
            dma((n_dom,)), dma((n_dom,)), dma((n_rep,)), dma((n_rep,)), dma, dma,
        ],
        compiler_params=params(2),
        name="return_gradients",
    )(gfeat, side, mix, send_rows)
    return pl.pallas_call(
        copy_out,
        out_shape=tuple(shape(a.shape, a.dtype) for a in results),
        in_specs=[VMEM] * 4,
        out_specs=(HBM,) * 4,
        scratch_shapes=[dma((4,))],
        compiler_params=pltpu.CompilerParams(vmem_limit_bytes=4 << 20),
        name="copy_out",
    )(*results)


def solution(mesh):
    in_specs = (
        P("dom", None),
        P(None, "dom"),
        P(),
        P(),
        P(),
        P(),
        P(None, "dom"),
        P(("dom", "rep")),
        P(("dom", "rep")),
        P(("dom", "rep")),
        P(None, ("dom", "rep")),
    )
    out_specs = (P("dom", None), P(None, "dom"), P(None, "dom"), P("dom", "rep"))
    body = functools.partial(on_device, mesh.shape["dom"], mesh.shape["rep"])
    return jax.shard_map(body, mesh=mesh, in_specs=in_specs, out_specs=out_specs, check_vma=False)
```
